256 devices in a mesh: expert: 128 (over z, x, y), dp: 2 (over core).
Axes of the slice: x: 4, y: 4, z: 8, core: 2. Of those that a mesh axis runs over, the one named last changes fastest.
Arguments:
- tokens: bfloat16 [32768, 7168], P(('expert', 'dp')), may hold values from -6 to 6
- cotangent: bfloat16 [32768, 7168], P(('expert', 'dp')), may hold values from -6 to 6
- logits: float32 [32768, 256], P(('expert', 'dp')), may hold values from -8 to 8
- expert_ids: int32 [32768, 8], P(('expert', 'dp')), may hold values from 0 to 255, all different within a row; in each aligned block of 128 rows (0 to 127, 128 to 255, ...) at most 5 rows name the same one
- gate_proj: bfloat16 [128, 7168, 128], P('expert'), may hold values from -0.0625 to 0.0625
- up_proj: bfloat16 [128, 7168, 128], P('expert'), may hold values from -0.0625 to 0.0625
- down_proj: bfloat16 [128, 128, 7168], P('expert'), may hold values from -0.125 to 0.125
Outputs:
- token_grad: bfloat16 [32768, 7168], P(('expert', 'dp'))
- logit_grad: float32 [32768, 256], P(('expert', 'dp'))
- down_grad: bfloat16 [128, 128, 7168], P('expert', None, 'dp')
The draws below stay inside these ranges and needn't reach their ends.
Inputs may be any that keep to these rules, and one draw needn't show every extreme that they name: `expert_ids`: each row names 8 different experts. Within the 128 rows of one device no expert is named more than 5 times, a bound that some block reaches.
All inputs are finite; a program needn't handle non-finite values.
Results may differ from the reference program's by a relative error of at most 0.012.
Values may be sent and summed in bfloat16 or wider, within the bound.
A program may use at most 192 MiB of HBM per device.

```python
import math
import jax
import jax.numpy as jnp
import numpy as np
from jax import lax

D = 7168
FF = 2048
TOP = 8
SPLIT = 16
TOK_DEV = 128
FF_DEV = 128
HELD = 8
EXPERTS = 256
CAP = 5
TOKENS = 32768


def steps_of(own_key, shape, cuts, smallest, top_value):
    factor_of, own = 1.0, jax.random.fold_in(own_key, 6)
    for axis_at, blocks in cuts:
        steps = jnp.exp(jax.random.uniform(jax.random.fold_in(own, axis_at), (blocks,), jnp.float32, smallest / len(cuts), top_value / len(cuts)))
        factor_of = factor_of * jnp.repeat(steps, shape[axis_at] // blocks).reshape([-1 if axis == axis_at else 1 for axis in range(len(shape))])
    return factor_of


def assign_block(rng, own, number, rows, count, top, limit, lean):
    order = jax.random.permutation(rng, count)
    heavy_load, common = shares(count, rows * top, limit, lean, True), shares(count, rows * top, limit, lean, False)
    places = jnp.arange(count)

    def named(sizes, offset_by):
        used = int((sizes > 0).sum())
        fixed = max(1, used // 4)
        passed = fixed + (places - fixed + offset_by * (used - fixed)) % max(1, count - fixed)
        return jnp.zeros((count,), jnp.int32).at[order[jnp.where(places < fixed, places, passed)]].set(jnp.asarray(sizes, jnp.int32))

    sizes = jnp.where(number % 4 == 0, named(heavy_load, number // 4), named(common, number - number // 4 - 1))
    mixed = jax.random.permutation(jax.random.fold_in(own, 3), count)
    giver, sink = mixed[0:count // 2 * 2:2], mixed[1:count // 2 * 2:2]
    slack = jnp.minimum(sizes[giver] - 1, limit - sizes[sink]) // 2
    slack = jnp.where((giver == order[0]) | (sink == order[0]) | (sizes[sink] == 0), 0, jnp.maximum(slack, 0))
    passed = jax.random.randint(jax.random.fold_in(own, 4), (count // 2,), 0, 1 << 20) % (slack + 1)
    sizes = sizes.at[giver].add(-passed).at[sink].add(passed)
    items = jnp.searchsorted(jnp.cumsum(sizes), jnp.arange(rows * top), side="right").astype(jnp.int32)
    grid = items.reshape(top, rows).T
    grid = grid[jax.random.permutation(jax.random.fold_in(own, 1), rows)]
    offset_by = jax.random.randint(jax.random.fold_in(own, 2), (rows, 1), 0, top)
    return jnp.take_along_axis(grid, (jnp.arange(top)[None, :] + offset_by) % top, axis=1)


def shares(amount, total, limit, skew, full):
    loads = [(1 << 20) // math.isqrt(grade ** skew) + 1 for grade in range(1, amount + 1)]
    largest = limit if full else min(limit, max(-(-total // amount), total * loads[0] // sum(loads)))
    least = 1 if total - largest >= amount - 1 else 0
    counts, rest = [largest] + [least] * (amount - 1), total - largest - least * (amount - 1)
    while rest > 0:
        movable = [i for i in range(1, amount) if counts[i] < largest] or [i for i in range(1, amount) if counts[i] < limit]
        mass, remaining = sum([loads[i] for i in movable]), rest
        for i in movable:
            more = min(limit - counts[i], max(1, remaining * loads[i] // mass), rest)
            counts[i] = counts[i] + more
            rest = rest - more
    return np.array(counts)


def normal_values(stream_key, extent, scale, reach, split=(), kind=jnp.bfloat16):
    factor_of = steps_of(stream_key, extent, split, -0.22, 0.18) if split else 1.0
    result = jax.random.normal(stream_key, extent, jnp.float32) * scale * factor_of
    return jnp.minimum(jnp.maximum(result, -reach), reach).astype(kind)


def setup_inputs(seed: int = 0) -> dict:
    streams_of = jax.random.split(jax.random.key(seed), 8)
    tokens = normal_values(streams_of[0], (TOKENS, D), 1.0, 6.0, ((0, 256),))
    cotangent = normal_values(streams_of[1], (TOKENS, D), 1.0, 6.0, ((0, 256),))
    logits = normal_values(streams_of[2], (TOKENS, EXPERTS), 2.0, 8.0, ((0, 256),), jnp.float32)
    expert_ids_keys = jax.random.split(jax.random.fold_in(streams_of[3], 1), TOKENS // TOK_DEV)
    expert_ids_turns = jax.random.permutation(jax.random.fold_in(streams_of[3], 3), TOKENS // TOK_DEV)
    expert_ids = jax.vmap(lambda own, number: assign_block(jax.random.fold_in(streams_of[3], 2), own, number, TOK_DEV, EXPERTS, TOP, CAP, 2))(expert_ids_keys, expert_ids_turns).reshape((TOKENS, TOP))
    gate_proj = normal_values(streams_of[4], (HELD * SPLIT, D, FF_DEV), D ** -0.5, 0.0625, ((0, 128),))
    up_proj = normal_values(streams_of[5], (HELD * SPLIT, D, FF_DEV), D ** -0.5, 0.0625, ((0, 128),))
    down_proj = normal_values(streams_of[6], (HELD * SPLIT, FF_DEV, D), FF ** -0.5, 0.125, ((0, 128),))
    return {"tokens": tokens, "cotangent": cotangent, "logits": logits, "expert_ids": expert_ids, "gate_proj": gate_proj, "up_proj": up_proj, "down_proj": down_proj}


SCALE = 2.5

def slot_ranks(block_ids, experts):
    flat = block_ids.reshape(-1)
    onehot = (flat[:, None] == jnp.arange(experts, dtype=jnp.int32)[None, :]).astype(jnp.int32)
    before = jnp.cumsum(onehot, axis=0) - onehot
    return lax.optimization_barrier(jnp.sum(before * onehot, axis=1)).astype(jnp.int32)

def router_weights(logits, expert_ids):
    experts = logits.shape[1]
    pick = (expert_ids[:, :, None] == jnp.arange(experts, dtype=jnp.int32)[None, None, :]).astype(jnp.float32)
    chosen = lax.optimization_barrier(jnp.sum(pick * jax.nn.sigmoid(logits)[:, None, :], axis=2))
    total = lax.optimization_barrier(jnp.sum(chosen, axis=1, keepdims=True))
    return (pick, chosen, total, SCALE * chosen / total)

def router_grad(pick, chosen, total, dweight):
    inner = lax.optimization_barrier(jnp.sum(dweight * chosen, axis=1, keepdims=True)) / total
    dchosen = SCALE / total * (dweight - inner)
    dlogit = dchosen * chosen * (1.0 - chosen)
    return lax.optimization_barrier(jnp.sum(pick * dlogit[:, :, None], axis=1))

def expert_forward(rows, gate, up):
    gated = jnp.dot(rows, gate, preferred_element_type=jnp.float32)
    upped = jnp.dot(rows, up, preferred_element_type=jnp.float32)
    sig = jax.nn.sigmoid(gated)
    active = gated * sig
    hidden = (active * upped).astype(jnp.bfloat16)
    return (gated, upped, sig, active, hidden)

def expert_backward(forward, cot, weight_b, gate, up, down):
    gated, upped, sig, active, hidden = forward
    contract = (((1,), (1,)), ((), ()))
    proj = lax.dot_general(cot, down, contract, preferred_element_type=jnp.float32)
    dots = lax.optimization_barrier(jnp.sum(hidden.astype(jnp.float32) * proj, axis=1)).astype(jnp.bfloat16)
    dhidden = weight_b.astype(jnp.float32)[:, None] * proj
    dgate = (dhidden * upped * sig * (1.0 + gated * (1.0 - sig))).astype(jnp.bfloat16)
    dup = (dhidden * active).astype(jnp.bfloat16)
    back = lax.dot_general(dgate, gate, contract, preferred_element_type=jnp.float32)
    back = back + lax.dot_general(dup, up, contract, preferred_element_type=jnp.float32)
    scaled = (weight_b.astype(jnp.float32)[:, None] * cot.astype(jnp.float32)).astype(jnp.bfloat16)
    dweight = lax.dot_general(hidden, scaled, (((0,), (0,)), ((), ())), preferred_element_type=jnp.float32)
    return (dots, back.astype(jnp.bfloat16), dweight)

def reference(tokens, cotangent, logits, expert_ids, gate_proj, up_proj, down_proj):
    held = gate_proj.shape[0] // SPLIT
    piece_width = gate_proj.shape[2]
    width = tokens.shape[1]
    experts = logits.shape[1]
    top = expert_ids.shape[1]
    total_tok = tokens.shape[0]
    sources = total_tok // TOK_DEV
    pick, chosen, total, weight = router_weights(logits, expert_ids)
    weight_b = weight.astype(jnp.bfloat16).reshape(-1)
    ranks = lax.map(lambda blk: slot_ranks(blk, experts), expert_ids.reshape(sources, TOK_DEV, top)).reshape(-1)
    flat_ids = expert_ids.reshape(-1)
    entry = jnp.arange(total_tok * top, dtype=jnp.int32)
    source = entry // (TOK_DEV * top)
    inside = flat_ids < held
    target = jnp.where(inside, flat_ids, held).astype(jnp.int32)
    column = (source * CAP + ranks).astype(jnp.int32)
    table = jnp.full((held, sources * CAP), -1, jnp.int32).at[target, column].set(entry, mode='drop')
    gates = gate_proj.reshape(held, SPLIT, width, piece_width)
    ups = up_proj.reshape(held, SPLIT, width, piece_width)
    downs = down_proj.reshape(held, SPLIT, piece_width, width)

    def one_expert(carry, inputs):
        back_sum, dots_all = carry
        slots, gate_e, up_e, down_e = inputs
        live = slots >= 0
        entry_safe = jnp.where(live, slots, 0).astype(jnp.int32)
        tok = (entry_safe // top).astype(jnp.int32)
        rows = jnp.where(live[:, None], tokens[tok], jnp.zeros((), jnp.bfloat16))
        cot = jnp.where(live[:, None], cotangent[tok], jnp.zeros((), jnp.bfloat16))
        wsl = jnp.where(live, weight_b[entry_safe], jnp.zeros((), jnp.bfloat16))

        def one_piece(acc, pieces):
            back_acc, dots_acc = acc
            gate, up, down = pieces
            forward = expert_forward(rows, gate, up)
            dots, back, dweight = expert_backward(forward, cot, wsl, gate, up, down)
            return ((back_acc + back.astype(jnp.float32), dots_acc + dots.astype(jnp.float32)), dweight.astype(jnp.bfloat16))
        start_acc = (jnp.zeros(rows.shape, jnp.float32), jnp.zeros((rows.shape[0],), jnp.float32))
        (back_acc, dots_acc), piece_grads = lax.scan(one_piece, start_acc, (gate_e, up_e, down_e))
        back_sum = back_sum.at[tok].add(jnp.where(live[:, None], back_acc, jnp.zeros((), jnp.float32)))
        dots_all = dots_all.at[entry_safe].add(jnp.where(live, dots_acc, jnp.zeros((), jnp.float32)))
        return ((back_sum, dots_all), piece_grads)
    start = (jnp.zeros((total_tok, width), jnp.float32), jnp.zeros((total_tok * top,), jnp.float32))
    (back_sum, dots_all), down_grad = lax.scan(one_expert, start, (table, gates, ups, downs))
    dweight_tk = jnp.where(inside, dots_all, jnp.zeros((), jnp.float32)).reshape(total_tok, top)
    logit_grad = router_grad(pick, chosen, total, dweight_tk)
    return (back_sum.astype(jnp.bfloat16), logit_grad, down_grad.reshape(held * SPLIT, piece_width, width))
```

```python
import jax
import jax.numpy as jnp
from jax import lax
from jax.experimental import pallas as pl
from jax.experimental.pallas import tpu as pltpu
from jax.sharding import PartitionSpec as P

NZ, NX, NY = 8, 4, 4
NS = NZ * NY
SCALE = 2.5
CAP = 5
SLOTS = NZ * CAP
PAD = 48
LAG = 4
MESH = pl.DeviceIdType.MESH
f32, bf16 = jnp.float32, jnp.bfloat16
NT = (((1,), (1,)), ((), ()))
TN = (((0,), (0,)), ((), ()))


def kernel(
    put_ref, putw_ref, take_ref, tok_hbm, cot_hbm, gate_hbm, up_hbm, down_hbm,
    tg_ref, dots_ref, dg_hbm,
    tok, cot, sendb, rx, xr, cr, wg, wu, wd, relay_g, relay_u, relay_d,
    part, own1, y1p, y1m, y2p, y2m, mid, bk, own2, x1p, x1m, x2p, x2m,
    retb, fin, dd, dsend, drecv, dout,
    lsem, wlsem, sem_a, sem_bp, sem_bm, sem_cp, sem_cm, wsem, rsem, psem,
    ysem, msem, xsem, fsem, ssem, dsem, osem,
):
    wide = xr.shape[1]
    half = wide // 2
    ffd = gate_hbm.shape[1]
    rows = NS * CAP
    e = lax.axis_index("expert")
    c = lax.axis_index("dp")
    z, x, y = e // (NX * NY), (e // NY) % NX, e % NY
    other = 1 - c
    at = lambda zz, xx, yy: zz * (NX * NY) + xx * NY + yy
    yp, ym, y2 = (y + 1) % NY, (y + 3) % NY, (y + 2) % NY
    xp, xm, x2 = (x + 1) % NX, (x + 3) % NX, (x + 2) % NX
    me = z * NY + y
    dev_yp, dev_ym = at(z, x, yp), at(z, x, ym)
    dev_xp, dev_xm = at(z, xp, y), at(z, xm, y)

    def remote(src, dst, recv, ex, dp=c):
        return pltpu.make_async_remote_copy(
            src_ref=src, dst_ref=dst, send_sem=ssem.at[0], recv_sem=recv,
            device_id=(ex, dp), device_id_type=MESH,
        )

    sent = []

    def send(src, dst, recv, ex, dp=c):
        cp = remote(src, dst, recv, ex, dp)
        cp.start()
        sent.append(cp)

    def arrived(dst, recv):
        remote(dst, dst, recv, dev_yp).wait_recv()

    ld_t = pltpu.make_async_copy(tok_hbm, tok, lsem.at[0])
    ld_c = pltpu.make_async_copy(cot_hbm, cot, lsem.at[1])
    ld_t.start()
    ld_c.start()
    r_own = pl.ds(pl.multiple_of(y * wide, wide), wide)
    l_own = pl.ds(pl.multiple_of(y * ffd, ffd), ffd)
    w_loads = [
        pltpu.make_async_copy(gate_hbm.at[r_own], wg.at[:, l_own], wlsem.at[0]),
        pltpu.make_async_copy(up_hbm.at[r_own], wu.at[:, l_own], wlsem.at[1]),
        pltpu.make_async_copy(down_hbm.at[:, r_own], wd.at[l_own], wlsem.at[2]),
    ]
    for cp in w_loads:
        cp.start()

    barrier = pltpu.get_barrier_semaphore()

    def greet(ex, dp):
        pl.semaphore_signal(barrier, inc=1, device_id=(ex, dp), device_id_type=MESH)

    @pl.loop(1, NS)
    def _(d):
        greet(at((z + d // NY) % NZ, x, (y + d % NY) % NY), c)

    greet(dev_xp, c)
    greet(dev_xm, c)
    for d in range(NY):
        greet(at(z, x, (y + d) % NY), other)

    fin[:, SLOTS:PAD] = jnp.zeros((NY, PAD - SLOTS, 2, fin.shape[3]), bf16)
    ld_t.wait()
    ld_c.wait()
    for yy in range(NY):
        cols = slice(yy * wide, (yy + 1) * wide)
        v = jnp.dot(put_ref[...], tok[:, cols], preferred_element_type=f32).astype(bf16)
        sendb[yy, 0] = v.reshape(PAD, 2, half)
        v = jnp.dot(putw_ref[...], cot[:, cols], preferred_element_type=f32).astype(bf16)
        sendb[yy, 1] = v.reshape(PAD, 2, half)

    pl.semaphore_wait(barrier, NS - 1 + 2 + NY)

    def a_copy(d):
        zz, yy = (z + d // NY) % NZ, (y + d % NY) % NY
        return remote(
            sendb.at[yy, :, pl.ds(zz * CAP, CAP)], rx.at[:, x, pl.ds(me * CAP, CAP)],
            sem_a.at[me], at(zz, x, yy),
        )

    own = pltpu.make_async_copy(
        sendb.at[y, :, pl.ds(z * CAP, CAP)], rx.at[:, x, pl.ds(me * CAP, CAP)], sem_a.at[me]
    )
    own.start()

    @pl.loop(1, NS)
    def _(d):
        a_copy(d).start()

    h = pl.ds(pl.multiple_of(c * half, half), half)

    def src_of(yy):
        r = pl.ds(pl.multiple_of(yy * wide + c * half, half), half)
        return (gate_hbm.at[r], up_hbm.at[r], down_hbm.at[:, r])

    def dst_of(yy, hh):
        l = pl.ds(pl.multiple_of(yy * ffd, ffd), ffd)
        return (wg.at[hh, l], wu.at[hh, l], wd.at[l, hh])

    relays = (relay_g, relay_u, relay_d)
    via = jnp.where(c == 0, dev_yp, dev_ym)
    came = jnp.where(c == 0, ym, yp)
    for i, s in enumerate(src_of(y2)):
        send(s, relays[i], rsem.at[i], via)
    for i, s in enumerate(src_of(yp)):
        send(s, dst_of(y, h)[i], wsem.at[y, i], dev_yp)
    for i, s in enumerate(src_of(ym)):
        send(s, dst_of(y, h)[i], wsem.at[y, i], dev_ym)

    def src_at(d):
        s = ((z + NZ - d // NY) % NZ) * NY + (y + NY - d % NY) % NY
        return s, pl.ds(s * CAP, CAP)

    def b_copies(d):
        s, r = src_at(d)
        blk = rx.at[:, x, r]
        return remote(blk, blk, sem_bp.at[s], dev_xp), remote(blk, blk, sem_bm.at[s], dev_xm)

    def c_copies(d):
        s, r = src_at(d)
        pb, mb = rx.at[0, xm, r], rx.at[1, xp, r]
        return remote(pb, pb, sem_cp.at[s], dev_xp), remote(mb, mb, sem_cm.at[s], dev_xm)

    def start_b(d):
        for cp in b_copies(d):
            cp.start()

    def start_c(d):
        s, r = src_at(d)
        arrived(rx.at[:, xm, r], sem_bp.at[s])
        arrived(rx.at[:, xp, r], sem_bm.at[s])
        for cp in c_copies(d):
            cp.start()

    def wait_a(d):
        s, r = src_at(d)
        arrived(rx.at[:, x, r], sem_a.at[s])

    own.wait()
    start_b(0)

    @pl.loop(1, LAG)
    def _(d):
        wait_a(d)
        start_b(d)

    @pl.loop(LAG, NS // 2)
    def _(d):
        wait_a(d)
        start_b(d)
        start_c(d - LAG)

    for i in range(3):
        arrived(relays[i], rsem.at[i])
        send(relays[i], dst_of(came, h)[i], wsem.at[came, i], via)

    @pl.loop(NS // 2, NS)
    def _(d):
        wait_a(d)
        start_b(d)
        start_c(d - LAG)

    @pl.loop(NS - LAG, NS)
    def _(d):
        start_c(d)

    for yy in (yp, ym, y2):
        for i in range(3):
            blk = dst_of(yy, h)[i]
            arrived(blk, wsem.at[yy, i])
            send(blk, blk, psem.at[yy, i], e, other)

    @pl.loop(0, NS)
    def _(d):
        s, r = src_at(d)
        arrived(rx.at[0, x2, r], sem_cp.at[s])
        arrived(rx.at[1, x2, r], sem_cm.at[s])

    @pl.loop(0, rows // 16)
    def _(i):
        r = pl.ds(i * 16, 16)
        for k in range(NX):
            o = pl.ds(pl.multiple_of(k * rows + i * 16, 16), 16)
            xr[o] = rx[0, k, r].reshape(16, wide)
            cr[o] = rx[1, k, r].reshape(16, wide)

    ho = pl.ds(pl.multiple_of(other * half, half), half)
    for cp in w_loads:
        cp.wait()
    for yy in (yp, ym, y2):
        for i in range(3):
            arrived(dst_of(yy, ho)[i], psem.at[yy, i])

    def reduce_scatter(compute, part, own_ref, hh, pos, dev_p, dev_m, b1p, b1m, b2p, b2m, sems, between):
        kp, km, kf = (pos + 1) % 4, (pos + 3) % 4, (pos + 2) % 4
        lo, hi = slice(0, hh), slice(hh, part.shape[2])
        compute(kf, None)
        send(part.at[kf, :, lo], b1p, sems.at[0], dev_p)
        send(part.at[kf, :, hi], b1m, sems.at[1], dev_m)
        compute(kp, None)
        send(part.at[kp, :, hi], b2p.at[:, hi], sems.at[2], dev_p)
        compute(km, None)
        send(part.at[km, :, lo], b2m.at[:, lo], sems.at[3], dev_m)
        compute(pos, own_ref)
        arrived(b1p, sems.at[0])
        part[kp, :, lo] = (part[kp, :, lo].astype(f32) + b1p[...].astype(f32)).astype(bf16)
        send(part.at[kp, :, lo], b2p.at[:, lo], sems.at[4], dev_p)
        arrived(b1m, sems.at[1])
        part[km, :, hi] = (part[km, :, hi].astype(f32) + b1m[...].astype(f32)).astype(bf16)
        send(part.at[km, :, hi], b2m.at[:, hi], sems.at[5], dev_m)
        between()
        arrived(b2p.at[:, hi], sems.at[2])
        arrived(b2m.at[:, lo], sems.at[3])
        arrived(b2p.at[:, lo], sems.at[4])
        arrived(b2m.at[:, hi], sems.at[5])

    ff = wg.shape[1]

    def forward(k, keep):
        r = pl.ds(pl.multiple_of(k * rows, 16), rows)
        xv, cv = xr[r], cr[r]
        vals = (
            jnp.dot(xv, wg[...], preferred_element_type=f32),
            jnp.dot(xv, wu[...], preferred_element_type=f32),
            lax.dot_general(cv, wd[...], NT, preferred_element_type=f32),
        )
        for i, v in enumerate(vals):
            if keep is None:
                part[k, :, i * ff : (i + 1) * ff] = v.astype(bf16)
            else:
                keep[:, i * ff : (i + 1) * ff] = v

    reduce_scatter(
        forward, part, own1, 3 * ff // 2, y, dev_yp, dev_ym, y1p, y1m, y2p, y2m, ysem, lambda: None
    )

    @pl.loop(0, rows // 16)
    def _(i):
        r = pl.ds(pl.multiple_of(i * 16, 16), 16)
        full = own1[r] + y2p[r].astype(f32) + y2m[r].astype(f32)
        g, u, pw = full[:, :ff], full[:, ff : 2 * ff], full[:, 2 * ff :]
        sig = jax.nn.sigmoid(g)
        act = g * sig
        hid = (act * u).astype(bf16)
        prod = hid.astype(f32) * pw
        lanes = prod[:, :128]
        for k in range(1, ff // 128):
            lanes = lanes + prod[:, k * 128 : (k + 1) * 128]
        mid[y, r, 0:ff] = hid
        mid[y, r, ff : 2 * ff] = (pw * u * sig * (1.0 + g * (1.0 - sig))).astype(bf16)
        mid[y, r, 2 * ff : 3 * ff] = (pw * act).astype(bf16)
        mid[y, r, 3 * ff : 3 * ff + 128] = lanes.astype(bf16)

    ca, cb = slice(0, 896), slice(896, mid.shape[2])
    block = lambda k, cols: mid.at[k, :, cols]
    send(block(y, ca), block(y, ca), msem.at[0], dev_yp)
    send(block(y, cb), block(y, cb), msem.at[1], dev_ym)
    send(block(y, cb), block(y, cb), msem.at[2], dev_yp)
    send(block(y, ca), block(y, ca), msem.at[3], dev_ym)
    arrived(block(ym, ca), msem.at[0])
    send(block(ym, ca), block(ym, ca), msem.at[4], dev_yp)
    arrived(block(yp, cb), msem.at[1])
    send(block(yp, cb), block(yp, cb), msem.at[5], dev_ym)
    arrived(block(ym, cb), msem.at[2])
    arrived(block(yp, ca), msem.at[3])
    arrived(block(y2, ca), msem.at[4])
    arrived(block(y2, cb), msem.at[5])

    def backward(k, keep):
        v = lax.dot_general(mid[k, :, ff : 2 * ff], wg[...], NT, preferred_element_type=f32)
        v = v + lax.dot_general(mid[k, :, 2 * ff : 3 * ff], wu[...], NT, preferred_element_type=f32)
        lanes = mid[k, :, 3 * ff : 3 * ff + 128]
        if keep is None:
            bk[k, :, :wide] = v.astype(bf16)
            bk[k, :, wide:] = lanes
        else:
            keep[:, :wide] = v
            keep[:, wide:] = lanes.astype(f32)

    mine = pl.ds(pl.multiple_of(c * (ff // 2), ff // 2), ff // 2)
    theirs = pl.ds(pl.multiple_of(other * (ff // 2), ff // 2), ff // 2)

    def down_part():
        for n in range(0, wide, 256):
            cols = slice(n, n + 256)
            acc = None
            for k in range(NX):
                v = lax.dot_general(
                    mid[k, :, 0:ff], cr[k * rows : (k + 1) * rows, cols], TN, preferred_element_type=f32
                )
                acc = v if acc is None else acc + v
            dd[:, cols] = acc
        dsend[...] = dd[theirs].astype(bf16)
        send(dsend, drecv, dsem.at[0], e, other)
        arrived(drecv, dsem.at[0])
        dout[...] = (dd[mine] + drecv[...].astype(f32)).astype(bf16)

    reduce_scatter(
        backward, bk, own2, 1024, x, dev_xp, dev_xm, x1p, x1m, x2p, x2m, xsem, down_part
    )

    @pl.loop(0, rows // 16)
    def _(i):
        r = pl.ds(pl.multiple_of(i * 16, 16), 16)
        full = own2[r] + x2p[r].astype(f32) + x2m[r].astype(f32)
        retb[pl.ds(i * 16, 16), :, 0:half] = full[:, :wide].astype(bf16).reshape(16, 2, half)
        lanes = jnp.concatenate([full[:, wide:], jnp.zeros((16, 128), f32)], axis=1).astype(bf16)
        retb[pl.ds(i * 16, 16), :, half : half + 128] = lanes.reshape(16, 2, 128)

    def f_copy(d):
        zz, yy = (z + d // NY) % NZ, (y + d % NY) % NY
        return remote(
            retb.at[pl.ds((zz * NY + yy) * CAP, CAP)], fin.at[y, pl.ds(z * CAP, CAP)],
            fsem.at[me], at(zz, x, yy),
        )

    back_own = pltpu.make_async_copy(
        retb.at[pl.ds(me * CAP, CAP)], fin.at[y, pl.ds(z * CAP, CAP)], fsem.at[me]
    )
    back_own.start()

    @pl.loop(1, NS)
    def _(d):
        f_copy(d).start()

    to_core = y // 2
    o_cols = pl.ds(pl.multiple_of((y % 2) * wide, wide), wide)
    for i in range(2):
        yy = 2 * c + i
        src = dout.at[pl.ds(i * ffd, ffd)]
        here = (yy == y) & (to_core == c)

        @pl.when(here)
        def _():
            pltpu.make_async_copy(src, dg_hbm.at[0, :, o_cols], osem.at[y % 2]).start()

        @pl.when(jnp.logical_not(here))
        def _():
            remote(src, dg_hbm.at[0, :, o_cols], osem.at[y % 2], at(z, x, yy), to_core).start()

    back_own.wait()

    @pl.loop(1, NS)
    def _(d):
        zz, yy = (z + NZ - d // NY) % NZ, (y + NY - d % NY) % NY
        arrived(fin.at[yy, pl.ds(zz * CAP, CAP)], fsem.at[zz * NY + yy])

    for yy in range(NY):
        v = fin[yy, :, :, 0:half].reshape(PAD, wide)
        tg_ref[:, yy * wide : (yy + 1) * wide] = jnp.dot(
            take_ref[...], v, preferred_element_type=f32
        ).astype(bf16)
    dots_ref[...] = fin[0, :, :, half : half + 128].reshape(PAD, 256)[:, :128].astype(f32)

    for i in range(2):
        arrived(dg_hbm.at[0, :, i * wide : (i + 1) * wide], osem.at[i])
    for cp in sent:
        cp.wait_send()

    @pl.loop(1, NS)
    def _(d):
        a_copy(d).wait_send()
        f_copy(d).wait_send()

    @pl.loop(0, NS)
    def _(d):
        for cp in (*b_copies(d), *c_copies(d)):
            cp.wait_send()

    for i in range(2):
        yy = 2 * c + i

        @pl.when(jnp.logical_not((yy == y) & (to_core == c)))
        def _():
            remote(dout.at[pl.ds(i * ffd, ffd)], dg_hbm.at[0, :, o_cols], osem.at[y % 2], at(z, x, yy), to_core).wait_send()


def exchange(put, putw, take, tokens, cotangent, gate, up, down):
    tok_count, width = tokens.shape
    ffd = gate.shape[1]
    wide, ff, rows = width // NY, NY * ffd, NS * CAP
    half = wide // 2
    n = NX * rows
    vm = pltpu.VMEM
    dma = pltpu.SemaphoreType.DMA
    scratch = [
        vm((tok_count, width), bf16), vm((tok_count, width), bf16),
        vm((NY, 2, PAD, 2, half), bf16), vm((2, NX, rows, 2, half), bf16),
        vm((n, wide), bf16), vm((n, wide), bf16),
        vm((wide, ff), bf16), vm((wide, ff), bf16), vm((ff, wide), bf16),
        vm((half, ffd), bf16), vm((half, ffd), bf16), vm((ffd, half), bf16),
        vm((NY, rows, 3 * ff), bf16), vm((rows, 3 * ff), f32),
        vm((rows, 3 * ff // 2), bf16), vm((rows, 3 * ff // 2), bf16),
        vm((rows, 3 * ff), bf16), vm((rows, 3 * ff), bf16),
        vm((NY, rows, 3 * ff + 128), bf16),
        vm((NX, rows, wide + 128), bf16), vm((rows, wide + 128), f32),
        vm((rows, 1024), bf16), vm((rows, wide + 128 - 1024), bf16),
        vm((rows, wide + 128), bf16), vm((rows, wide + 128), bf16),
        vm((rows, 2, half + 128), bf16), vm((NY, PAD, 2, half + 128), bf16),
        vm((ff, wide), f32), vm((ff // 2, wide), bf16), vm((ff // 2, wide), bf16), vm((ff // 2, wide), bf16),
        dma((2,)), dma((3,)), dma((NS,)), dma((NS,)), dma((NS,)), dma((NS,)), dma((NS,)),
        dma((NY, 3)), dma((3,)), dma((NY, 3)),
        dma((6,)), dma((6,)), dma((6,)), dma((NS,)), dma((1,)), dma((1,)), dma((2,)),
    ]
    v, a = pl.BlockSpec(memory_space=pltpu.VMEM), pl.BlockSpec(memory_space=pl.ANY)
    return pl.pallas_call(
        kernel,
        out_shape=(
            jax.ShapeDtypeStruct((tok_count, width), bf16),
            jax.ShapeDtypeStruct((PAD, 128), f32),
            jax.ShapeDtypeStruct((1, ffd, width // 2), bf16),
        ),
        in_specs=[v, v, v, a, a, a, a, a],
        out_specs=(v, v, a),
        scratch_shapes=scratch,
        compiler_params=pltpu.CompilerParams(
            collective_id=0, has_side_effects=True, vmem_limit_bytes=63 * 1024 * 1024
        ),
    )(put, putw, take, tokens, cotangent, gate, up, down)


def per_device(tokens, cotangent, logits, expert_ids, gate_proj, up_proj, down_proj):
    tok_count = expert_ids.shape[0]
    experts = logits.shape[1]
    pick = (expert_ids[:, :, None] == jnp.arange(experts, dtype=jnp.int32)[None, None, :]).astype(f32)
    chosen = jnp.sum(pick * jax.nn.sigmoid(logits)[:, None, :], axis=2)
    total = jnp.sum(chosen, axis=1, keepdims=True)
    weight_b = (SCALE * chosen / total).astype(bf16)
    live = expert_ids[:, :, None] == jnp.arange(NZ, dtype=jnp.int32)[None, None, :]
    member = jnp.any(live, axis=1)
    w_te = jnp.sum(jnp.where(live, weight_b.astype(f32)[:, :, None], 0.0), axis=1)
    rank = jnp.dot(jnp.tril(jnp.ones((tok_count, tok_count), f32), -1), member.astype(f32))
    place = member[:, :, None] & (rank[:, :, None] == jnp.arange(CAP, dtype=f32)[None, None, :])
    place = place.reshape(tok_count, SLOTS)
    place_f = jnp.pad(place.astype(f32), ((0, 0), (0, PAD - SLOTS)))
    place_w = jnp.pad(
        jnp.where(place, jnp.repeat(w_te, CAP, axis=1), 0.0), ((0, 0), (0, PAD - SLOTS))
    )
    token_grad, lanes, dd = exchange(
        place_f.T.astype(bf16), place_w.T.astype(bf16), place_f.astype(bf16),
        tokens, cotangent, gate_proj[0], up_proj[0], down_proj[0],
    )
    dots = jnp.sum(lanes, axis=1)[:SLOTS].reshape(NZ, CAP)
    d_te = jnp.sum(place.astype(f32).reshape(tok_count, NZ, CAP) * dots[None], axis=2)
    dweight = jnp.sum(jnp.where(live, d_te[:, None, :], 0.0), axis=2) / weight_b.astype(f32)
    inner = jnp.sum(dweight * chosen, axis=1, keepdims=True) / total
    dchosen = SCALE / total * (dweight - inner)
    logit_grad = jnp.sum(pick * (dchosen * chosen * (1.0 - chosen))[:, :, None], axis=1)
    return token_grad, logit_grad, dd


def solution(mesh):
    rows = P(("expert", "dp"), None)
    mats = P("expert", None, None)
    return jax.shard_map(
        per_device,
        mesh=mesh,
        in_specs=(rows, rows, rows, rows, mats, mats, mats),
        out_specs=(rows, rows, P("expert", None, "dp")),
        check_vma=False,
    )
```

```python
import jax
import jax.numpy as jnp
from jax import lax
from jax.experimental import pallas as pl
from jax.experimental.pallas import tpu as pltpu
from jax.sharding import PartitionSpec as P

NZ, NX, NY = 8, 4, 4
NS = NZ * NY
SCALE = 2.5
CAP = 5
SLOTS = NZ * CAP
PAD = 48
LAG = 4
NB = 2
STOP = 99
MESH = pl.DeviceIdType.MESH
f32, bf16 = jnp.float32, jnp.bfloat16
NT = (((1,), (1,)), ((), ()))
TN = (((0,), (0,)), ((), ()))


def z_step(q):
    return jnp.where(q % 2 == 1, (q + 1) // 2, (NZ - q // 2) % NZ)


def iota(shape, dim):
    return lax.broadcasted_iota(jnp.int32, shape, dim)


def slot_map():
    e, s = iota((128, 128), 0), iota((128, 128), 1)
    return ((s >= CAP * e) & (s < CAP * (e + 1)) & (e < NZ)).astype(f32).astype(bf16)


def weights_of(named, total):
    return jnp.where(named > 0.0, SCALE * named / total, 0.0).astype(bf16)


def router(logits_ref, ids_ref):
    rows = logits_ref.shape[0]
    ids = jnp.transpose(ids_ref[...].astype(f32))
    lanes = iota(logits_ref.shape, 1).astype(f32)
    hit = lanes == ids[:, 0:1]
    for k in range(1, ids.shape[1]):
        hit = hit | (lanes == ids[:, k : k + 1])
    named = jnp.where(hit, jax.nn.sigmoid(logits_ref[...]), 0.0)
    total = jnp.sum(named, axis=1, keepdims=True)
    held = named[:, :128]
    slots = slot_map()
    member = jnp.dot((held > 0.0).astype(f32).astype(bf16), slots, preferred_element_type=f32)
    spread = jnp.dot(weights_of(held, total), slots, preferred_element_type=f32)
    earlier = (iota((rows, rows), 0) > iota((rows, rows), 1)).astype(f32).astype(bf16)
    rank = jnp.dot(earlier, member.astype(bf16), preferred_element_type=f32)
    lane = iota((rows, 128), 1)
    first = jnp.zeros((rows, 128), jnp.int32)
    for j in range(1, NZ):
        first = first + CAP * (lane >= CAP * j).astype(jnp.int32)
    place = jnp.where(rank == (lane - first).astype(f32), member, 0.0)
    return named, total, place, place * spread


def kernel(
    logits_ref, ids_ref, tok_hbm, cot_hbm, gate_hbm, up_hbm, down_hbm,
    named_ref, total_ref, take_ref, fin, dg_hbm,
    tok, cot, sendb, rx, xr, cr, wg, wu, wd, relay_g, relay_u, relay_d,
    part, y1p, y1m, y2p, y2m, mid, bk, x1p, x1m, x2p, x2m,
    retb, dl, dt, dd, dsend, drecv, dout,
    lsem, wlsem, sem_a, sem_bp, sem_bm, sem_cp, sem_cm, wsem, rsem, psem,
    ysem, msem, xsem, fsem, ssem, dsem, osem, tsem,
):
    wide = xr.shape[1]
    half = wide // 2
    ffd = gate_hbm.shape[1]
    ff = wg.shape[1]
    rows = NS * CAP
    step = rows // NB
    batch = NX * step
    e = lax.axis_index("expert")
    c = lax.axis_index("dp")
    z, x, y = e // (NX * NY), (e // NY) % NX, e % NY
    other = 1 - c
    at = lambda zz, xx, yy: zz * (NX * NY) + xx * NY + yy
    yp, ym, y2 = (y + 1) % NY, (y + 3) % NY, (y + 2) % NY
    xp, xm, x2 = (x + 1) % NX, (x + 3) % NX, (x + 2) % NX
    dev_yp, dev_ym = at(z, x, yp), at(z, x, ym)
    dev_xp, dev_xm = at(z, xp, y), at(z, xm, y)
    dev_t = at(z, y, x)

    def remote(src, dst, recv, ex, dp=c):
        return pltpu.make_async_remote_copy(
            src_ref=src, dst_ref=dst, send_sem=ssem.at[0], recv_sem=recv,
            device_id=(ex, dp), device_id_type=MESH,
        )

    sent = []

    def send(src, dst, recv, ex, dp=c):
        cp = remote(src, dst, recv, ex, dp)
        cp.start()
        sent.append(cp)

    def arrived(dst, recv):
        remote(dst, dst, recv, dev_yp).wait_recv()

    ld_t = pltpu.make_async_copy(tok_hbm, tok, lsem.at[0])
    ld_c = pltpu.make_async_copy(cot_hbm, cot, lsem.at[1])
    ld_t.start()
    ld_c.start()

    barrier = pltpu.get_barrier_semaphore()

    def greet(ex, dp):
        pl.semaphore_signal(barrier, inc=1, device_id=(ex, dp), device_id_type=MESH)

    @pl.loop(1, NS)
    def _(d):
        greet(at((z + d // NY) % NZ, x, (y + d % NY) % NY), c)

    greet(dev_xp, c)
    greet(dev_xm, c)
    for d in range(NY):
        greet(at(z, x, (y + d) % NY), other)

    @pl.when(x != y)
    def _():
        greet(dev_t, c)

    r_own = pl.ds(pl.multiple_of(y * wide, wide), wide)
    l_own = pl.ds(pl.multiple_of(y * ffd, ffd), ffd)
    w_loads = [
        pltpu.make_async_copy(gate_hbm.at[r_own], wg.at[:, l_own], wlsem.at[0]),
        pltpu.make_async_copy(up_hbm.at[r_own], wu.at[:, l_own], wlsem.at[1]),
        pltpu.make_async_copy(down_hbm.at[:, r_own], wd.at[l_own], wlsem.at[2]),
    ]
    for cp in w_loads:
        cp.start()

    named, total, place, place_w = router(logits_ref, ids_ref)
    named_ref[...] = named
    total_ref[...] = jnp.broadcast_to(total, total_ref.shape)
    take_ref[...] = place.astype(bf16)
    put, put_w = place[:, :PAD].astype(bf16), place_w[:, :PAD].astype(bf16)
    pl.semaphore_wait(barrier, NS - 1 + 2 + NY + jnp.where(x == y, 0, 1))

    h = pl.ds(pl.multiple_of(c * half, half), half)

    def src_of(yy):
        r = pl.ds(pl.multiple_of(yy * wide + c * half, half), half)
        return (gate_hbm.at[r], up_hbm.at[r], down_hbm.at[:, r])

    def dst_of(yy, hh):
        l = pl.ds(pl.multiple_of(yy * ffd, ffd), ffd)
        return (wg.at[hh, l], wu.at[hh, l], wd.at[l, hh])

    relays = (relay_g, relay_u, relay_d)
    via = jnp.where(c == 0, dev_yp, dev_ym)
    came = jnp.where(c == 0, ym, yp)
    send(src_of(y2)[2], relays[2], rsem.at[2], via)
    ld_t.wait()
    ld_c.wait()
    for yy in range(NY):
        cols = slice(yy * wide, (yy + 1) * wide)
        v = lax.dot_general(put, tok[:, cols], TN, preferred_element_type=f32).astype(bf16)
        sendb[yy, 0] = v[:SLOTS].reshape(SLOTS, 2, half)
        v = lax.dot_general(put_w, cot[:, cols], TN, preferred_element_type=f32).astype(bf16)
        sendb[yy, 1] = v[:SLOTS].reshape(SLOTS, 2, half)

    def a_copy(d):
        q = d // NY
        zz, yy, s = (z + z_step(q)) % NZ, (y + d % NY) % NY, q * NY + y
        return remote(
            sendb.at[yy, :, pl.ds(zz * CAP, CAP)], rx.at[:, x, pl.ds(s * CAP, CAP)],
            sem_a.at[s], at(zz, x, yy),
        )

    own = pltpu.make_async_copy(
        sendb.at[y, :, pl.ds(z * CAP, CAP)], rx.at[:, x, pl.ds(y * CAP, CAP)], sem_a.at[y]
    )
    own.start()

    @pl.loop(1, NS)
    def _(d):
        a_copy(d).start()

    for i in (0, 1):
        send(src_of(y2)[i], relays[i], rsem.at[i], via)
    for i, s in enumerate(src_of(yp)):
        send(s, dst_of(y, h)[i], wsem.at[y, i], dev_yp)
    for i, s in enumerate(src_of(ym)):
        send(s, dst_of(y, h)[i], wsem.at[y, i], dev_ym)

    def src_at(d):
        s = (d // NY) * NY + (y + NY - d % NY) % NY
        return s, pl.ds(s * CAP, CAP)

    def b_copies(d):
        s, r = src_at(d)
        blk = rx.at[:, x, r]
        return remote(blk, blk, sem_bp.at[s], dev_xp), remote(blk, blk, sem_bm.at[s], dev_xm)

    def c_copies(d):
        s, r = src_at(d)
        pb, mb = rx.at[0, xm, r], rx.at[1, xp, r]
        return remote(pb, pb, sem_cp.at[s], dev_xp), remote(mb, mb, sem_cm.at[s], dev_xm)

    def start_b(d):
        for cp in b_copies(d):
            cp.start()

    def start_c(d):
        s, r = src_at(d)
        arrived(rx.at[:, xm, r], sem_bp.at[s])
        arrived(rx.at[:, xp, r], sem_bm.at[s])
        for cp in c_copies(d):
            cp.start()

    def wait_a(d):
        s, r = src_at(d)
        arrived(rx.at[:, x, r], sem_a.at[s])

    own.wait()
    start_b(0)

    @pl.loop(1, LAG)
    def _(d):
        wait_a(d)
        start_b(d)

    @pl.loop(LAG, 8)
    def _(d):
        wait_a(d)
        start_b(d)
        start_c(d - LAG)

    arrived(relays[2], rsem.at[2])
    send(relays[2], dst_of(came, h)[2], wsem.at[came, 2], via)

    @pl.loop(8, 14)
    def _(d):
        wait_a(d)
        start_b(d)
        start_c(d - LAG)

    arrived(relays[0], rsem.at[0])
    send(relays[0], dst_of(came, h)[0], wsem.at[came, 0], via)

    @pl.loop(14, 20)
    def _(d):
        wait_a(d)
        start_b(d)
        start_c(d - LAG)

    arrived(relays[1], rsem.at[1])
    send(relays[1], dst_of(came, h)[1], wsem.at[came, 1], via)

    @pl.loop(20, NS)
    def _(d):
        wait_a(d)
        start_b(d)
        start_c(d - LAG)


    def swap(yy):
        for i in range(3):
            blk = dst_of(yy, h)[i]
            arrived(blk, wsem.at[yy, i])
            send(blk, blk, psem.at[yy, i], e, other)

    swap(yp)
    swap(ym)

    @pl.loop(NS - LAG, NS)
    def _(d):
        start_c(d)

    def unpack(b):
        @pl.loop(0, step // 16)
        def _(i):
            o = pl.multiple_of(b * step + i * 16, 16)
            for k in range(NX):
                r = pl.ds(pl.multiple_of(b * batch + k * step + i * 16, 16), 16)
                xr[r] = rx[0, k, pl.ds(o, 16)].reshape(16, wide)
                cr[r] = rx[1, k, pl.ds(o, 16)].reshape(16, wide)

    def wait_c(b):
        @pl.loop(b * (NS // NB), (b + 1) * (NS // NB))
        def _(d):
            s, r = src_at(d)
            arrived(rx.at[0, x2, r], sem_cp.at[s])
            arrived(rx.at[1, x2, r], sem_cm.at[s])

    wait_c(0)
    unpack(0)

    swap(y2)
    ho = pl.ds(pl.multiple_of(other * half, half), half)
    for cp in w_loads:
        cp.wait()
    for yy in (yp, ym, y2):
        for i in range(3):
            arrived(dst_of(yy, ho)[i], psem.at[yy, i])

    def chunk(k, b):
        return pl.ds(pl.multiple_of(b * batch + k * step, 16), step)

    class Scatter:
        def __init__(self, part, pos, dev_p, dev_m, b1p, b1m, b2p, b2m, sems):
            self.part, self.pos = part, pos
            self.devs, self.bufs, self.sems = (dev_p, dev_m), (b1p, b1m, b2p, b2m), sems
            self.kp, self.km, self.kf = (pos + 1) % 4, (pos + 3) % 4, (pos + 2) % 4
            w = part.shape[1]
            self.lo, self.hi = slice(0, w // 2), slice(w // 2, w)

        def start(self, b):
            r = slice(b * step, (b + 1) * step)
            b1p, b1m, b2p, b2m = self.bufs
            (p, m), lo, hi, sem = self.devs, self.lo, self.hi, self.sems
            far, kp, km = chunk(self.kf, b), chunk(self.kp, b), chunk(self.km, b)
            send(self.part.at[far, lo], b1p.at[r], sem.at[b, 0], p)
            send(self.part.at[far, hi], b1m.at[r], sem.at[b, 1], m)
            send(self.part.at[kp, hi], b2p.at[r, hi], sem.at[b, 2], p)
            send(self.part.at[km, lo], b2m.at[r, lo], sem.at[b, 3], m)

        def onward(self, b):
            r = slice(b * step, (b + 1) * step)
            b1p, b1m, b2p, b2m = self.bufs
            (p, m), lo, hi, sem = self.devs, self.lo, self.hi, self.sems
            for buf, k, cols, i, to, dev in (
                (b1p, self.kp, lo, 0, b2p, p), (b1m, self.km, hi, 1, b2m, m),
            ):
                arrived(buf.at[r], sem.at[b, i])
                c = chunk(k, b)
                self.part[c, cols] = (self.part[c, cols].astype(f32) + buf[r].astype(f32)).astype(bf16)
                send(self.part.at[c, cols], to.at[r, cols], sem.at[b, 4 + i], dev)

        def finish(self, b):
            r = slice(b * step, (b + 1) * step)
            _, _, b2p, b2m = self.bufs
            arrived(b2p.at[r, self.hi], self.sems.at[b, 2])
            arrived(b2m.at[r, self.lo], self.sems.at[b, 3])
            arrived(b2p.at[r, self.lo], self.sems.at[b, 4])
            arrived(b2m.at[r, self.hi], self.sems.at[b, 5])

    def forward(b):
        r = slice(b * batch, (b + 1) * batch)
        part[r, 0:ff] = jnp.dot(xr[r], wg[...], preferred_element_type=f32).astype(bf16)
        part[r, ff : 2 * ff] = jnp.dot(xr[r], wu[...], preferred_element_type=f32).astype(bf16)
        part[r, 2 * ff : 3 * ff] = lax.dot_general(
            cr[r], wd[...], NT, preferred_element_type=f32
        ).astype(bf16)

    def activate(b):
        @pl.loop(0, step // 16)
        def _(i):
            r = pl.ds(pl.multiple_of(b * step + i * 16, 16), 16)
            mr = pl.ds(pl.multiple_of(b * batch + y * step + i * 16, 16), 16)
            full = part[mr].astype(f32) + y2p[r].astype(f32) + y2m[r].astype(f32)
            g, u, pw = full[:, :ff], full[:, ff : 2 * ff], full[:, 2 * ff :]
            sig = jax.nn.sigmoid(g)
            act = g * sig
            hid = (act * u).astype(bf16)
            prod = hid.astype(f32) * pw
            lanes = prod[:, :128]
            for k in range(1, ff // 128):
                lanes = lanes + prod[:, k * 128 : (k + 1) * 128]
            mid[mr, 0:ff] = hid
            mid[mr, ff : 2 * ff] = (pw * u * sig * (1.0 + g * (1.0 - sig))).astype(bf16)
            mid[mr, 2 * ff : 3 * ff] = (pw * act).astype(bf16)
            top = lanes.astype(bf16)
            low = lanes - top.astype(f32)
            both = jnp.concatenate([top.astype(f32), low], axis=1).astype(bf16)
            dl[pl.ds(b * step + i * 16, 16)] = both.reshape(16, 2, 128)

    m_lo, m_hi = slice(0, 3 * ff // 2), slice(3 * ff // 2, 3 * ff)

    def block(k, b, cols):
        return mid.at[chunk(k, b), cols]

    def gather_start(b):
        for i, (cols, dev) in enumerate(((m_lo, dev_yp), (m_hi, dev_ym), (m_hi, dev_yp), (m_lo, dev_ym))):
            send(block(y, b, cols), block(y, b, cols), msem.at[b, i], dev)

    def gather_onward(b):
        arrived(block(ym, b, m_lo), msem.at[b, 0])
        send(block(ym, b, m_lo), block(ym, b, m_lo), msem.at[b, 4], dev_yp)
        arrived(block(yp, b, m_hi), msem.at[b, 1])
        send(block(yp, b, m_hi), block(yp, b, m_hi), msem.at[b, 5], dev_ym)

    def gather_finish(b):
        arrived(block(ym, b, m_hi), msem.at[b, 2])
        arrived(block(yp, b, m_lo), msem.at[b, 3])
        arrived(block(y2, b, m_lo), msem.at[b, 4])
        arrived(block(y2, b, m_hi), msem.at[b, 5])

    def backward(b):
        r = slice(b * batch, (b + 1) * batch)
        v = lax.dot_general(mid[r, ff : 2 * ff], wg[...], NT, preferred_element_type=f32)
        v = v + lax.dot_general(mid[r, 2 * ff : 3 * ff], wu[...], NT, preferred_element_type=f32)
        bk[r] = v.astype(bf16)

    def home(b):
        @pl.loop(0, step // 16)
        def _(i):
            o = pl.multiple_of(b * step + i * 16, 16)
            r = pl.ds(o, 16)
            mr = pl.ds(pl.multiple_of(b * batch + x * step + i * 16, 16), 16)
            full = bk[mr].astype(f32) + x2p[r].astype(f32) + x2m[r].astype(f32)
            retb[r, :, 0:half] = full.astype(bf16).reshape(16, 2, half)
            retb[r, :, half : half + 128] = dt[r]

        lo, hi = b * (NS // NB), (b + 1) * (NS // NB)

        @pl.loop(max(lo, 1), hi)
        def _(d):
            f_copy(d).start()

    def f_copy(d):
        s, r = src_at(d)
        return remote(
            retb.at[r], fin.at[y, pl.ds(z * CAP, CAP)], fsem.at[z * NY + y],
            at((z + NZ - z_step(d // NY)) % NZ, x, (y + NY - d % NY) % NY),
        )

    mine = pl.ds(pl.multiple_of(c * (ff // 2), ff // 2), ff // 2)
    theirs = pl.ds(pl.multiple_of(other * (ff // 2), ff // 2), ff // 2)
    to_core = y // 2
    o_cols = pl.ds(pl.multiple_of((y % 2) * wide, wide), wide)

    def out_copy(i):
        return remote(
            dout.at[pl.ds(i * ffd, ffd)], dg_hbm.at[0, :, o_cols], osem.at[y % 2],
            at(z, x, 2 * c + i), to_core,
        )

    def down_half(b):
        r = slice(b * batch, (b + 1) * batch)
        v = lax.dot_general(mid[r, 0:ff], cr[r], TN, preferred_element_type=f32)
        dd[...] = v if b == batches[0] else dd[...] + v

    fwd = Scatter(part, y, dev_yp, dev_ym, y1p, y1m, y2p, y2m, ysem)
    bwd = Scatter(bk, x, dev_xp, dev_xm, x1p, x1m, x2p, x2m, xsem)
    batches = tuple(range(NB))

    if STOP == 1:
        wait_c(1)
        unpack(1)
    if STOP > 1:
        forward(0)
        fwd.start(0)
        wait_c(1)
        unpack(1)
        forward(1)
        fwd.onward(0)
        fwd.start(1)
        fwd.onward(1)
        for b in batches:
            fwd.finish(b)
            activate(b)
            if STOP > 2:
                gather_start(b)

    if STOP > 2:
        dots_here = pltpu.make_async_copy(dl, dt, tsem.at[0])
        dots_there = remote(dl, dt, tsem.at[0], dev_t)

        @pl.when(x == y)
        def _():
            dots_here.start()

        @pl.when(x != y)
        def _():
            dots_there.start()

        first, last = batches[0], batches[-1]
        gather_onward(first)
        gather_finish(first)
        if STOP > 3:
            backward(first)
            bwd.start(first)
        gather_onward(last)
        if STOP > 3:
            down_half(first)
            bwd.onward(first)
        gather_finish(last)
        if STOP > 3:
            backward(last)
            bwd.start(last)
        arrived(dt, tsem.at[0])

    if STOP > 3:
        down_half(last)
        dsend[...] = dd[theirs].astype(bf16)
        send(dsend, drecv, dsem.at[0], e, other)
        bwd.onward(last)

    if STOP > 3:
        arrived(drecv, dsem.at[0])
        dout[...] = (dd[mine] + drecv[...].astype(f32)).astype(bf16)
        for i in range(2):
            here = (2 * c + i == y) & (to_core == c)

            @pl.when(here)
            def _():
                pltpu.make_async_copy(
                    dout.at[pl.ds(i * ffd, ffd)], dg_hbm.at[0, :, o_cols], osem.at[y % 2]
                ).start()

            @pl.when(jnp.logical_not(here))
            def _():
                out_copy(i).start()

    for b in batches:
        if STOP > 3:
            bwd.finish(b)
        if STOP > 4:
            home(b)

    if STOP > 4:
        back_own = pltpu.make_async_copy(
            retb.at[pl.ds(y * CAP, CAP)], fin.at[y, pl.ds(z * CAP, CAP)], fsem.at[z * NY + y]
        )
        back_own.start()
        back_own.wait()

        @pl.loop(1, NS)
        def _(d):
            zz, yy = (z + d // NY) % NZ, (y + d % NY) % NY
            arrived(fin.at[yy, pl.ds(zz * CAP, CAP)], fsem.at[zz * NY + yy])

        @pl.loop(1, NS)
        def _(d):
            f_copy(d).wait_send()

    for cp in sent:
        cp.wait_send()

    @pl.loop(1, NS)
    def _(d):
        a_copy(d).wait_send()

    @pl.loop(0, NS)
    def _(d):
        for cp in (*b_copies(d), *c_copies(d)):
            cp.wait_send()

    if STOP > 2:
        @pl.when(x != y)
        def _():
            dots_there.wait_send()

    if STOP > 3:
        for i in range(2):
            arrived(dg_hbm.at[0, :, i * wide : (i + 1) * wide], osem.at[i])

            @pl.when(jnp.logical_not((2 * c + i == y) & (to_core == c)))
            def _():
                out_copy(i).wait_send()


def exchange(logits, ids, tokens, cotangent, gate, up, down):
    tok_count, width = tokens.shape
    ffd = gate.shape[1]
    wide, ff, rows = width // NY, NY * ffd, NS * CAP
    half = wide // 2
    n = NX * rows
    vm = pltpu.VMEM
    dma = pltpu.SemaphoreType.DMA
    scratch = [
        vm((tok_count, width), bf16), vm((tok_count, width), bf16),
        vm((NY, 2, SLOTS, 2, half), bf16), vm((2, NX, rows, 2, half), bf16),
        vm((n, wide), bf16), vm((n, wide), bf16),
        vm((wide, ff), bf16), vm((wide, ff), bf16), vm((ff, wide), bf16),
        vm((half, ffd), bf16), vm((half, ffd), bf16), vm((ffd, half), bf16),
        vm((n, 3 * ff), bf16),
        vm((rows, 3 * ff // 2), bf16), vm((rows, 3 * ff // 2), bf16),
        vm((rows, 3 * ff), bf16), vm((rows, 3 * ff), bf16),
        vm((n, 3 * ff), bf16),
        vm((n, wide), bf16),
        vm((rows, half), bf16), vm((rows, half), bf16),
        vm((rows, wide), bf16), vm((rows, wide), bf16),
        vm((rows, 2, half + 128), bf16), vm((rows, 2, 128), bf16), vm((rows, 2, 128), bf16),
        vm((ff, wide), f32), vm((ff // 2, wide), bf16), vm((ff // 2, wide), bf16), vm((ff // 2, wide), bf16),
        dma((2,)), dma((3,)), dma((NS,)), dma((NS,)), dma((NS,)), dma((NS,)), dma((NS,)),
        dma((NY, 3)), dma((3,)), dma((NY, 3)),
        dma((NB, 6)), dma((NB, 6)), dma((NB, 6)), dma((NS,)), dma((1,)), dma((1,)), dma((2,)), dma((1,)),
    ]
    v, a = pl.BlockSpec(memory_space=pltpu.VMEM), pl.BlockSpec(memory_space=pl.ANY)
    return pl.pallas_call(
        kernel,
        out_shape=(
            jax.ShapeDtypeStruct(logits.shape, f32),
            jax.ShapeDtypeStruct((tok_count, 128), f32),
            jax.ShapeDtypeStruct((tok_count, 128), bf16),
            jax.ShapeDtypeStruct((NY, SLOTS, 2, half + 128), bf16),
            jax.ShapeDtypeStruct((1, ffd, width // 2), bf16),
        ),
        in_specs=[v, v, a, a, a, a, a],
        out_specs=(v, v, v, a, a),
        scratch_shapes=scratch,
        compiler_params=pltpu.CompilerParams(
            collective_id=0, has_side_effects=True, vmem_limit_bytes=62 * 1024 * 1024
        ),
        name="exchange",
    )(logits, ids, tokens, cotangent, gate, up, down)


def closing(named_ref, total_ref, take_ref, fin_ref, dg_in, tg_ref, lg_ref, dg_ref, acc):
    b = pl.program_id(0)
    half = fin_ref.shape[3] - 128
    dg_ref[...] = dg_in[...]
    v = fin_ref[0, :, :, 0:half].reshape(SLOTS, 2 * half)
    tg_ref[...] = jnp.dot(take_ref[:, :SLOTS], v, preferred_element_type=f32).astype(bf16)
    d = fin_ref[0, :, :, half : half + 128].reshape(SLOTS, 256).astype(f32)
    d = d[:, :128] + d[:, 128:]

    @pl.when(b == 0)
    def _():
        acc[...] = d

    @pl.when(b > 0)
    def _():
        acc[...] += d

    @pl.when(b == NY - 1)
    def _():
        dots = jnp.broadcast_to(jnp.sum(acc[...], axis=1, keepdims=True), (SLOTS, 128))
        top = dots.astype(bf16)
        low = (dots - top.astype(f32)).astype(bf16)
        slots = jnp.transpose(slot_map().astype(f32))[:SLOTS].astype(bf16)
        take = take_ref[:, :SLOTS]
        got = jnp.dot(take, slots * top, preferred_element_type=f32)
        got = got + jnp.dot(take, slots * low, preferred_element_type=f32)
        named, total = named_ref[...], total_ref[:, 0:1]
        held = named[:, :128]
        weight = weights_of(held, total).astype(f32)
        dweight = jnp.where(weight > 0.0, got / jnp.where(weight > 0.0, weight, 1.0), 0.0)
        inner = jnp.sum(dweight * held, axis=1, keepdims=True) / total
        rest = named[:, 128:]
        scale = SCALE / total
        lg_ref[:, :128] = scale * (dweight - inner) * held * (1.0 - held)
        lg_ref[:, 128:] = scale * (0.0 - inner) * rest * (1.0 - rest)


def per_device(tokens, cotangent, logits, expert_ids, gate_proj, up_proj, down_proj):
    tok_count, width = tokens.shape
    wide = width // NY
    ids = expert_ids.T
    ffd = gate_proj.shape[2]
    named, total, take, fin, dg = exchange(
        logits, ids, tokens, cotangent, gate_proj[0], up_proj[0], down_proj[0]
    )
    whole = lambda s: pl.BlockSpec(s, lambda b: (0,) * len(s))
    return pl.pallas_call(
        closing,
        grid=(NY,),
        out_shape=(
            jax.ShapeDtypeStruct(tokens.shape, bf16),
            jax.ShapeDtypeStruct(logits.shape, f32),
            jax.ShapeDtypeStruct(dg.shape, bf16),
        ),
        in_specs=[
            whole(named.shape), whole(total.shape), whole(take.shape),
            pl.BlockSpec((1,) + fin.shape[1:], lambda b: (b, 0, 0, 0)),
            pl.BlockSpec((1, ffd, wide // 2), lambda b: (0, 0, b)),
        ],
        out_specs=(
            pl.BlockSpec((tok_count, wide), lambda b: (0, b)),
            whole(logits.shape),
            pl.BlockSpec((1, ffd, wide // 2), lambda b: (0, 0, b)),
        ),
        scratch_shapes=[pltpu.VMEM((SLOTS, 128), f32)],
        name="closing",
    )(named, total, take, fin, dg)


def solution(mesh):
    rows = P(("expert", "dp"), None)
    mats = P("expert", None, None)
    return jax.shard_map(
        per_device,
        mesh=mesh,
        in_specs=(rows, rows, rows, rows, mats, mats, mats),
        out_specs=(rows, rows, P("expert", None, "dp")),
        check_vma=False,
    )
```

```python
import jax
import jax.numpy as jnp
from jax import lax
from jax.experimental import pallas as pl
from jax.experimental.pallas import tpu as pltpu
from jax.sharding import PartitionSpec as P

NZ, NX, NY = 8, 4, 4
NS = NZ * NY
SCALE = 2.5
CAP = 5
SLOTS = NZ * CAP
PAD = 48
LAG = 4
NB = 2
MESH = pl.DeviceIdType.MESH
f32, bf16 = jnp.float32, jnp.bfloat16
NT = (((1,), (1,)), ((), ()))
TN = (((0,), (0,)), ((), ()))


def z_step(q):
    return jnp.where(q % 2 == 1, (q + 1) // 2, (NZ - q // 2) % NZ)


def iota(shape, dim):
    return lax.broadcasted_iota(jnp.int32, shape, dim)


def slot_map():
    e, s = iota((128, 128), 0), iota((128, 128), 1)
    return ((s >= CAP * e) & (s < CAP * (e + 1)) & (e < NZ)).astype(f32).astype(bf16)


def weights_of(named, total):
    return jnp.where(named > 0.0, SCALE * named / total, 0.0).astype(bf16)


def router(logits_ref, ids_ref):
    rows = logits_ref.shape[0]
    ids = jnp.transpose(ids_ref[...].astype(f32))
    lanes = iota(logits_ref.shape, 1).astype(f32)
    hit = lanes == ids[:, 0:1]
    for k in range(1, ids.shape[1]):
        hit = hit | (lanes == ids[:, k : k + 1])
    named = jnp.where(hit, jax.nn.sigmoid(logits_ref[...]), 0.0)
    total = jnp.sum(named, axis=1, keepdims=True)
    held = named[:, :128]
    slots = slot_map()
    member = jnp.dot((held > 0.0).astype(f32).astype(bf16), slots, preferred_element_type=f32)
    spread = jnp.dot(weights_of(held, total), slots, preferred_element_type=f32)
    earlier = (iota((rows, rows), 0) > iota((rows, rows), 1)).astype(f32).astype(bf16)
    rank = jnp.dot(earlier, member.astype(bf16), preferred_element_type=f32)
    lane = iota((rows, 128), 1)
    first = jnp.zeros((rows, 128), jnp.int32)
    for j in range(1, NZ):
        first = first + CAP * (lane >= CAP * j).astype(jnp.int32)
    place = jnp.where(rank == (lane - first).astype(f32), member, 0.0)
    return named, total, place, place * spread


def kernel(
    logits_ref, ids_ref, tok_hbm, cot_hbm, gate_hbm, up_hbm, down_hbm,
    named_ref, total_ref, take_ref, fin, dg_hbm,
    tok, cot, sendb, rx, xr, cr, wg, wu, wd, relay_g, relay_u, relay_d,
    part, y1p, y1m, y2p, y2m, mid, bk, x1p, x1m, x2p, x2m,
    retb, dl, dt, dd, dsend, drecv, dout,
    lsem, wlsem, sem_a, sem_bp, sem_bm, sem_cp, sem_cm, wsem, rsem, psem,
    ysem, msem, xsem, fsem, ssem, dsem, osem, tsem,
):
    wide = xr.shape[1]
    half = wide // 2
    ffd = gate_hbm.shape[1]
    ff = wg.shape[1]
    rows = NS * CAP
    step = rows // NB
    batch = NX * step
    e = lax.axis_index("expert")
    c = lax.axis_index("dp")
    z, x, y = e // (NX * NY), (e // NY) % NX, e % NY
    other = 1 - c
    at = lambda zz, xx, yy: zz * (NX * NY) + xx * NY + yy
    yp, ym, y2 = (y + 1) % NY, (y + 3) % NY, (y + 2) % NY
    xp, xm, x2 = (x + 1) % NX, (x + 3) % NX, (x + 2) % NX
    dev_yp, dev_ym = at(z, x, yp), at(z, x, ym)
    dev_xp, dev_xm = at(z, xp, y), at(z, xm, y)
    dev_t = at(z, y, x)

    def remote(src, dst, recv, ex, dp=c):
        return pltpu.make_async_remote_copy(
            src_ref=src, dst_ref=dst, send_sem=ssem.at[0], recv_sem=recv,
            device_id=(ex, dp), device_id_type=MESH,
        )

    sent = []

    def send(src, dst, recv, ex, dp=c):
        cp = remote(src, dst, recv, ex, dp)
        cp.start()
        sent.append(cp)

    def arrived(dst, recv):
        remote(dst, dst, recv, dev_yp).wait_recv()

    ld_t = pltpu.make_async_copy(tok_hbm, tok, lsem.at[0])
    ld_c = pltpu.make_async_copy(cot_hbm, cot, lsem.at[1])
    ld_t.start()
    ld_c.start()

    barrier = pltpu.get_barrier_semaphore()

    def greet(ex, dp):
        pl.semaphore_signal(barrier, inc=1, device_id=(ex, dp), device_id_type=MESH)

    @pl.loop(1, NS)
    def _(d):
        greet(at((z + d // NY) % NZ, x, (y + d % NY) % NY), c)

    greet(dev_xp, c)
    greet(dev_xm, c)
    for d in range(NY):
        greet(at(z, x, (y + d) % NY), other)

    @pl.when(x != y)
    def _():
        greet(dev_t, c)

    r_own = pl.ds(pl.multiple_of(y * wide, wide), wide)
    l_own = pl.ds(pl.multiple_of(y * ffd, ffd), ffd)
    w_loads = [
        pltpu.make_async_copy(gate_hbm.at[r_own], wg.at[:, l_own], wlsem.at[0]),
        pltpu.make_async_copy(up_hbm.at[r_own], wu.at[:, l_own], wlsem.at[1]),
        pltpu.make_async_copy(down_hbm.at[:, r_own], wd.at[l_own], wlsem.at[2]),
    ]
    for cp in w_loads:
        cp.start()

    named, total, place, place_w = router(logits_ref, ids_ref)
    named_ref[...] = named
    total_ref[...] = jnp.broadcast_to(total, total_ref.shape)
    take_ref[...] = place.astype(bf16)
    put, put_w = place[:, :PAD].astype(bf16), place_w[:, :PAD].astype(bf16)
    pl.semaphore_wait(barrier, NS - 1 + 2 + NY + jnp.where(x == y, 0, 1))

    h = pl.ds(pl.multiple_of(c * half, half), half)

    def src_of(yy):
        r = pl.ds(pl.multiple_of(yy * wide + c * half, half), half)
        return (gate_hbm.at[r], up_hbm.at[r], down_hbm.at[:, r])

    def dst_of(yy, hh):
        l = pl.ds(pl.multiple_of(yy * ffd, ffd), ffd)
        return (wg.at[hh, l], wu.at[hh, l], wd.at[l, hh])

    relays = (relay_g, relay_u, relay_d)
    via = jnp.where(c == 0, dev_yp, dev_ym)
    came = jnp.where(c == 0, ym, yp)
    send(src_of(y2)[2], relays[2], rsem.at[2], via)
    ld_t.wait()
    ld_c.wait()
    for yy in range(NY):
        cols = slice(yy * wide, (yy + 1) * wide)
        v = lax.dot_general(put, tok[:, cols], TN, preferred_element_type=f32).astype(bf16)
        sendb[yy, 0] = v[:SLOTS].reshape(SLOTS, 2, half)
        v = lax.dot_general(put_w, cot[:, cols], TN, preferred_element_type=f32).astype(bf16)
        sendb[yy, 1] = v[:SLOTS].reshape(SLOTS, 2, half)

    def a_copy(d):
        q = d // NY
        zz, yy, s = (z + z_step(q)) % NZ, (y + d % NY) % NY, q * NY + y
        return remote(
            sendb.at[yy, :, pl.ds(zz * CAP, CAP)], rx.at[:, x, pl.ds(s * CAP, CAP)],
            sem_a.at[s], at(zz, x, yy),
        )

    own = pltpu.make_async_copy(
        sendb.at[y, :, pl.ds(z * CAP, CAP)], rx.at[:, x, pl.ds(y * CAP, CAP)], sem_a.at[y]
    )
    own.start()

    @pl.loop(1, NS)
    def _(d):
        a_copy(d).start()

    for i in (0, 1):
        send(src_of(y2)[i], relays[i], rsem.at[i], via)
    for i, s in enumerate(src_of(yp)):
        send(s, dst_of(y, h)[i], wsem.at[y, i], dev_yp)
    for i, s in enumerate(src_of(ym)):
        send(s, dst_of(y, h)[i], wsem.at[y, i], dev_ym)

    def src_at(d):
        s = (d // NY) * NY + (y + NY - d % NY) % NY
        return s, pl.ds(s * CAP, CAP)

    def b_copies(d):
        s, r = src_at(d)
        blk = rx.at[:, x, r]
        return remote(blk, blk, sem_bp.at[s], dev_xp), remote(blk, blk, sem_bm.at[s], dev_xm)

    def c_copies(d):
        s, r = src_at(d)
        pb, mb = rx.at[0, xm, r], rx.at[1, xp, r]
        return remote(pb, pb, sem_cp.at[s], dev_xp), remote(mb, mb, sem_cm.at[s], dev_xm)

    def start_b(d):
        for cp in b_copies(d):
            cp.start()

    def start_c(d):
        s, r = src_at(d)
        arrived(rx.at[:, xm, r], sem_bp.at[s])
        arrived(rx.at[:, xp, r], sem_bm.at[s])
        for cp in c_copies(d):
            cp.start()

    def wait_a(d):
        s, r = src_at(d)
        arrived(rx.at[:, x, r], sem_a.at[s])

    own.wait()
    start_b(0)

    @pl.loop(1, LAG)
    def _(d):
        wait_a(d)
        start_b(d)

    @pl.loop(LAG, 8)
    def _(d):
        wait_a(d)
        start_b(d)
        start_c(d - LAG)

    arrived(relays[2], rsem.at[2])
    send(relays[2], dst_of(came, h)[2], wsem.at[came, 2], via)

    @pl.loop(8, 14)
    def _(d):
        wait_a(d)
        start_b(d)
        start_c(d - LAG)

    arrived(relays[0], rsem.at[0])
    send(relays[0], dst_of(came, h)[0], wsem.at[came, 0], via)

    @pl.loop(14, 20)
    def _(d):
        wait_a(d)
        start_b(d)
        start_c(d - LAG)

    arrived(relays[1], rsem.at[1])
    send(relays[1], dst_of(came, h)[1], wsem.at[came, 1], via)

    @pl.loop(20, NS)
    def _(d):
        wait_a(d)
        start_b(d)
        start_c(d - LAG)


    def swap(yy):
        for i in range(3):
            blk = dst_of(yy, h)[i]
            arrived(blk, wsem.at[yy, i])
            send(blk, blk, psem.at[yy, i], e, other)

    swap(yp)
    swap(ym)

    @pl.loop(NS - LAG, NS)
    def _(d):
        start_c(d)

    def unpack(b):
        @pl.loop(0, step // 16)
        def _(i):
            o = pl.multiple_of(b * step + i * 16, 16)
            for k in range(NX):
                r = pl.ds(pl.multiple_of(b * batch + k * step + i * 16, 16), 16)
                xr[r] = rx[0, k, pl.ds(o, 16)].reshape(16, wide)
                cr[r] = rx[1, k, pl.ds(o, 16)].reshape(16, wide)

    def wait_c(b):
        @pl.loop(b * (NS // NB), (b + 1) * (NS // NB))
        def _(d):
            s, r = src_at(d)
            arrived(rx.at[0, x2, r], sem_cp.at[s])
            arrived(rx.at[1, x2, r], sem_cm.at[s])

    wait_c(0)
    unpack(0)

    swap(y2)
    ho = pl.ds(pl.multiple_of(other * half, half), half)
    for cp in w_loads:
        cp.wait()
    for yy in (yp, ym, y2):
        for i in range(3):
            arrived(dst_of(yy, ho)[i], psem.at[yy, i])

    def chunk(k, b):
        return pl.ds(pl.multiple_of(b * batch + k * step, 16), step)

    class Scatter:
        def __init__(self, part, pos, dev_p, dev_m, b1p, b1m, b2p, b2m, sems):
            self.part, self.pos = part, pos
            self.devs, self.bufs, self.sems = (dev_p, dev_m), (b1p, b1m, b2p, b2m), sems
            self.kp, self.km, self.kf = (pos + 1) % 4, (pos + 3) % 4, (pos + 2) % 4
            w = part.shape[1]
            self.lo, self.hi = slice(0, w // 2), slice(w // 2, w)

        def start(self, b):
            r = slice(b * step, (b + 1) * step)
            b1p, b1m, b2p, b2m = self.bufs
            (p, m), lo, hi, sem = self.devs, self.lo, self.hi, self.sems
            far, kp, km = chunk(self.kf, b), chunk(self.kp, b), chunk(self.km, b)
            send(self.part.at[far, lo], b1p.at[r], sem.at[b, 0], p)
            send(self.part.at[far, hi], b1m.at[r], sem.at[b, 1], m)
            send(self.part.at[kp, hi], b2p.at[r, hi], sem.at[b, 2], p)
            send(self.part.at[km, lo], b2m.at[r, lo], sem.at[b, 3], m)

        def onward(self, b):
            r = slice(b * step, (b + 1) * step)
            b1p, b1m, b2p, b2m = self.bufs
            (p, m), lo, hi, sem = self.devs, self.lo, self.hi, self.sems
            for buf, k, cols, i, to, dev in (
                (b1p, self.kp, lo, 0, b2p, p), (b1m, self.km, hi, 1, b2m, m),
            ):
                arrived(buf.at[r], sem.at[b, i])
                c = chunk(k, b)
                self.part[c, cols] = (self.part[c, cols].astype(f32) + buf[r].astype(f32)).astype(bf16)
                send(self.part.at[c, cols], to.at[r, cols], sem.at[b, 4 + i], dev)

        def finish(self, b):
            r = slice(b * step, (b + 1) * step)
            _, _, b2p, b2m = self.bufs
            arrived(b2p.at[r, self.hi], self.sems.at[b, 2])
            arrived(b2m.at[r, self.lo], self.sems.at[b, 3])
            arrived(b2p.at[r, self.lo], self.sems.at[b, 4])
            arrived(b2m.at[r, self.hi], self.sems.at[b, 5])

    def forward(b):
        r = slice(b * batch, (b + 1) * batch)
        part[r, 0:ff] = jnp.dot(xr[r], wg[...], preferred_element_type=f32).astype(bf16)
        part[r, ff : 2 * ff] = jnp.dot(xr[r], wu[...], preferred_element_type=f32).astype(bf16)
        part[r, 2 * ff : 3 * ff] = lax.dot_general(
            cr[r], wd[...], NT, preferred_element_type=f32
        ).astype(bf16)

    def activate(b):
        @pl.loop(0, step // 16)
        def _(i):
            r = pl.ds(pl.multiple_of(b * step + i * 16, 16), 16)
            mr = pl.ds(pl.multiple_of(b * batch + y * step + i * 16, 16), 16)
            full = part[mr].astype(f32) + y2p[r].astype(f32) + y2m[r].astype(f32)
            g, u, pw = full[:, :ff], full[:, ff : 2 * ff], full[:, 2 * ff :]
            sig = jax.nn.sigmoid(g)
            act = g * sig
            hid = (act * u).astype(bf16)
            prod = hid.astype(f32) * pw
            lanes = prod[:, :128]
            for k in range(1, ff // 128):
                lanes = lanes + prod[:, k * 128 : (k + 1) * 128]
            mid[mr, 2 * ff : 3 * ff] = hid
            mid[mr, 0:ff] = (pw * u * sig * (1.0 + g * (1.0 - sig))).astype(bf16)
            mid[mr, ff : 2 * ff] = (pw * act).astype(bf16)
            top = lanes.astype(bf16)
            low = lanes - top.astype(f32)
            both = jnp.concatenate([top.astype(f32), low], axis=1).astype(bf16)
            dl[pl.ds(b * step + i * 16, 16)] = both.reshape(16, 2, 128)

    gather_cols = (
        (slice(0, ff), slice(ff, 2 * ff)),
        (slice(2 * ff, 5 * ff // 2), slice(5 * ff // 2, 3 * ff)),
    )

    def block(k, b, cols):
        return mid.at[chunk(k, b), cols]

    def gather_start(b, g):
        lo, hi = gather_cols[g]
        for i, (cols, dev) in enumerate(((lo, dev_yp), (hi, dev_ym), (hi, dev_yp), (lo, dev_ym))):
            send(block(y, b, cols), block(y, b, cols), msem.at[b, 6 * g + i], dev)

    def gather_onward(b, g):
        lo, hi = gather_cols[g]
        arrived(block(ym, b, lo), msem.at[b, 6 * g])
        send(block(ym, b, lo), block(ym, b, lo), msem.at[b, 6 * g + 4], dev_yp)
        arrived(block(yp, b, hi), msem.at[b, 6 * g + 1])
        send(block(yp, b, hi), block(yp, b, hi), msem.at[b, 6 * g + 5], dev_ym)

    def gather_finish(b, g):
        lo, hi = gather_cols[g]
        arrived(block(ym, b, hi), msem.at[b, 6 * g + 2])
        arrived(block(yp, b, lo), msem.at[b, 6 * g + 3])
        arrived(block(y2, b, lo), msem.at[b, 6 * g + 4])
        arrived(block(y2, b, hi), msem.at[b, 6 * g + 5])

    def backward(b):
        r = slice(b * batch, (b + 1) * batch)
        v = lax.dot_general(mid[r, 0:ff], wg[...], NT, preferred_element_type=f32)
        v = v + lax.dot_general(mid[r, ff : 2 * ff], wu[...], NT, preferred_element_type=f32)
        bk[r] = v.astype(bf16)

    def home(b):
        @pl.loop(0, step // 16)
        def _(i):
            o = pl.multiple_of(b * step + i * 16, 16)
            r = pl.ds(o, 16)
            mr = pl.ds(pl.multiple_of(b * batch + x * step + i * 16, 16), 16)
            full = bk[mr].astype(f32) + x2p[r].astype(f32) + x2m[r].astype(f32)
            retb[r, :, 0:half] = full.astype(bf16).reshape(16, 2, half)
            retb[r, :, half : half + 128] = dt[r]

        lo, hi = b * (NS // NB), (b + 1) * (NS // NB)

        @pl.loop(max(lo, 1), hi)
        def _(d):
            f_copy(d).start()

    def f_copy(d):
        s, r = src_at(d)
        return remote(
            retb.at[r], fin.at[y, pl.ds(z * CAP, CAP)], fsem.at[z * NY + y],
            at((z + NZ - z_step(d // NY)) % NZ, x, (y + NY - d % NY) % NY),
        )

    mine = pl.ds(pl.multiple_of(c * (ff // 2), ff // 2), ff // 2)
    theirs = pl.ds(pl.multiple_of(other * (ff // 2), ff // 2), ff // 2)
    to_core = y // 2
    o_cols = pl.ds(pl.multiple_of((y % 2) * wide, wide), wide)

    def out_copy(i):
        return remote(
            dout.at[pl.ds(i * ffd, ffd)], dg_hbm.at[0, :, o_cols], osem.at[y % 2],
            at(z, x, 2 * c + i), to_core,
        )

    def down_half(b):
        r = slice(b * batch, (b + 1) * batch)
        v = lax.dot_general(mid[r, 2 * ff : 3 * ff], cr[r], TN, preferred_element_type=f32)
        dd[...] = v if b == batches[0] else dd[...] + v

    fwd = Scatter(part, y, dev_yp, dev_ym, y1p, y1m, y2p, y2m, ysem)
    bwd = Scatter(bk, x, dev_xp, dev_xm, x1p, x1m, x2p, x2m, xsem)
    batches = tuple(range(NB))

    forward(0)
    fwd.start(0)
    wait_c(1)
    unpack(1)
    forward(1)
    fwd.onward(0)
    fwd.start(1)
    fwd.onward(1)
    for b in batches:
        fwd.finish(b)
        activate(b)
        gather_start(b, 0)

    dots_here = pltpu.make_async_copy(dl, dt, tsem.at[0])
    dots_there = remote(dl, dt, tsem.at[0], dev_t)

    @pl.when(x == y)
    def _():
        dots_here.start()

    @pl.when(x != y)
    def _():
        dots_there.start()

    gather_onward(0, 0)
    gather_start(0, 1)
    gather_onward(1, 0)
    gather_start(1, 1)
    gather_finish(0, 0)
    backward(0)
    bwd.start(0)
    gather_onward(0, 1)
    gather_finish(1, 0)
    backward(1)
    bwd.onward(0)
    bwd.start(1)
    gather_onward(1, 1)
    gather_finish(0, 1)
    down_half(0)
    gather_finish(1, 1)
    down_half(1)
    dsend[...] = dd[theirs].astype(bf16)
    send(dsend, drecv, dsem.at[0], e, other)
    arrived(dt, tsem.at[0])
    bwd.onward(1)
    bwd.finish(0)
    home(0)
    arrived(drecv, dsem.at[0])
    dout[...] = (dd[mine] + drecv[...].astype(f32)).astype(bf16)
    for i in range(2):
        here = (2 * c + i == y) & (to_core == c)

        @pl.when(here)
        def _():
            pltpu.make_async_copy(
                dout.at[pl.ds(i * ffd, ffd)], dg_hbm.at[0, :, o_cols], osem.at[y % 2]
            ).start()

        @pl.when(jnp.logical_not(here))
        def _():
            out_copy(i).start()

    bwd.finish(1)
    home(1)

    back_own = pltpu.make_async_copy(
        retb.at[pl.ds(y * CAP, CAP)], fin.at[y, pl.ds(z * CAP, CAP)], fsem.at[z * NY + y]
    )
    back_own.start()
    back_own.wait()

    @pl.loop(1, NS)
    def _(d):
        zz, yy = (z + d // NY) % NZ, (y + d % NY) % NY
        arrived(fin.at[yy, pl.ds(zz * CAP, CAP)], fsem.at[zz * NY + yy])

    @pl.loop(1, NS)
    def _(d):
        f_copy(d).wait_send()

    for cp in sent:
        cp.wait_send()

    @pl.loop(1, NS)
    def _(d):
        a_copy(d).wait_send()

    @pl.loop(0, NS)
    def _(d):
        for cp in (*b_copies(d), *c_copies(d)):
            cp.wait_send()

    @pl.when(x != y)
    def _():
        dots_there.wait_send()

    for i in range(2):
        arrived(dg_hbm.at[0, :, i * wide : (i + 1) * wide], osem.at[i])

        @pl.when(jnp.logical_not((2 * c + i == y) & (to_core == c)))
        def _():
            out_copy(i).wait_send()


def exchange(logits, ids, tokens, cotangent, gate, up, down):
    tok_count, width = tokens.shape
    ffd = gate.shape[1]
    wide, ff, rows = width // NY, NY * ffd, NS * CAP
    half = wide // 2
    n = NX * rows
    vm = pltpu.VMEM
    dma = pltpu.SemaphoreType.DMA
    scratch = [
        vm((tok_count, width), bf16), vm((tok_count, width), bf16),
        vm((NY, 2, SLOTS, 2, half), bf16), vm((2, NX, rows, 2, half), bf16),
        vm((n, wide), bf16), vm((n, wide), bf16),
        vm((wide, ff), bf16), vm((wide, ff), bf16), vm((ff, wide), bf16),
        vm((half, ffd), bf16), vm((half, ffd), bf16), vm((ffd, half), bf16),
        vm((n, 3 * ff), bf16),
        vm((rows, 3 * ff // 2), bf16), vm((rows, 3 * ff // 2), bf16),
        vm((rows, 3 * ff), bf16), vm((rows, 3 * ff), bf16),
        vm((n, 3 * ff), bf16),
        vm((n, wide), bf16),
        vm((rows, half), bf16), vm((rows, half), bf16),
        vm((rows, wide), bf16), vm((rows, wide), bf16),
        vm((rows, 2, half + 128), bf16), vm((rows, 2, 128), bf16), vm((rows, 2, 128), bf16),
        vm((ff, wide), f32), vm((ff // 2, wide), bf16), vm((ff // 2, wide), bf16), vm((ff // 2, wide), bf16),
        dma((2,)), dma((3,)), dma((NS,)), dma((NS,)), dma((NS,)), dma((NS,)), dma((NS,)),
        dma((NY, 3)), dma((3,)), dma((NY, 3)),
        dma((NB, 6)), dma((NB, 12)), dma((NB, 6)), dma((NS,)), dma((1,)), dma((1,)), dma((2,)), dma((1,)),
    ]
    v, a = pl.BlockSpec(memory_space=pltpu.VMEM), pl.BlockSpec(memory_space=pl.ANY)
    return pl.pallas_call(
        kernel,
        out_shape=(
            jax.ShapeDtypeStruct(logits.shape, f32),
            jax.ShapeDtypeStruct((tok_count, 128), f32),
            jax.ShapeDtypeStruct((tok_count, 128), bf16),
            jax.ShapeDtypeStruct((NY, SLOTS, 2, half + 128), bf16),
            jax.ShapeDtypeStruct((1, ffd, width // 2), bf16),
        ),
        in_specs=[v, v, a, a, a, a, a],
        out_specs=(v, v, v, a, a),
        scratch_shapes=scratch,
        compiler_params=pltpu.CompilerParams(
            collective_id=0, has_side_effects=True, vmem_limit_bytes=62 * 1024 * 1024
        ),
        name="exchange",
    )(logits, ids, tokens, cotangent, gate, up, down)


def closing(named_ref, total_ref, take_ref, fin_ref, dg_in, tg_ref, lg_ref, dg_ref, acc):
    b = pl.program_id(0)
    half = fin_ref.shape[3] - 128
    dg_ref[...] = dg_in[...]
    v = fin_ref[0, :, :, 0:half].reshape(SLOTS, 2 * half)
    tg_ref[...] = jnp.dot(take_ref[:, :SLOTS], v, preferred_element_type=f32).astype(bf16)
    d = fin_ref[0, :, :, half : half + 128].reshape(SLOTS, 256).astype(f32)
    d = d[:, :128] + d[:, 128:]

    @pl.when(b == 0)
    def _():
        acc[...] = d

    @pl.when(b > 0)
    def _():
        acc[...] += d

    @pl.when(b == NY - 1)
    def _():
        dots = jnp.broadcast_to(jnp.sum(acc[...], axis=1, keepdims=True), (SLOTS, 128))
        top = dots.astype(bf16)
        low = (dots - top.astype(f32)).astype(bf16)
        slots = jnp.transpose(slot_map().astype(f32))[:SLOTS].astype(bf16)
        take = take_ref[:, :SLOTS]
        got = jnp.dot(take, slots * top, preferred_element_type=f32)
        got = got + jnp.dot(take, slots * low, preferred_element_type=f32)
        named, total = named_ref[...], total_ref[:, 0:1]
        held = named[:, :128]
        weight = weights_of(held, total).astype(f32)
        dweight = jnp.where(weight > 0.0, got / jnp.where(weight > 0.0, weight, 1.0), 0.0)
        inner = jnp.sum(dweight * held, axis=1, keepdims=True) / total
        rest = named[:, 128:]
        scale = SCALE / total
        lg_ref[:, :128] = scale * (dweight - inner) * held * (1.0 - held)
        lg_ref[:, 128:] = scale * (0.0 - inner) * rest * (1.0 - rest)


def per_device(tokens, cotangent, logits, expert_ids, gate_proj, up_proj, down_proj):
    tok_count, width = tokens.shape
    wide = width // NY
    ids = expert_ids.T
    ffd = gate_proj.shape[2]
    named, total, take, fin, dg = exchange(
        logits, ids, tokens, cotangent, gate_proj[0], up_proj[0], down_proj[0]
    )
    whole = lambda s: pl.BlockSpec(s, lambda b: (0,) * len(s))
    return pl.pallas_call(
        closing,
        grid=(NY,),
        out_shape=(
            jax.ShapeDtypeStruct(tokens.shape, bf16),
            jax.ShapeDtypeStruct(logits.shape, f32),
            jax.ShapeDtypeStruct(dg.shape, bf16),
        ),
        in_specs=[
            whole(named.shape), whole(total.shape), whole(take.shape),
            pl.BlockSpec((1,) + fin.shape[1:], lambda b: (b, 0, 0, 0)),
            pl.BlockSpec((1, ffd, wide // 2), lambda b: (0, 0, b)),
        ],
        out_specs=(
            pl.BlockSpec((tok_count, wide), lambda b: (0, b)),
            whole(logits.shape),
            pl.BlockSpec((1, ffd, wide // 2), lambda b: (0, 0, b)),
        ),
        scratch_shapes=[pltpu.VMEM((SLOTS, 128), f32)],
        name="closing",
    )(named, total, take, fin, dg)


def solution(mesh):
    rows = P(("expert", "dp"), None)
    mats = P("expert", None, None)
    return jax.shard_map(
        per_device,
        mesh=mesh,
        in_specs=(rows, rows, rows, rows, mats, mats, mats),
        out_specs=(rows, rows, P("expert", None, "dp")),
        check_vma=False,
    )
```

```python
import jax
import jax.numpy as jnp
from jax import lax
from jax.experimental import pallas as pl
from jax.experimental.pallas import tpu as pltpu
from jax.sharding import PartitionSpec as P

NZ, NX, NY = 8, 4, 4
NS = NZ * NY
SCALE = 2.5
CAP = 5
SLOTS = NZ * CAP
PAD = 48
LAG = 4
NB = 2
MESH = pl.DeviceIdType.MESH
f32, bf16 = jnp.float32, jnp.bfloat16
NT = (((1,), (1,)), ((), ()))
TN = (((0,), (0,)), ((), ()))


def z_step(q):
    return jnp.where(q % 2 == 1, (q + 1) // 2, (NZ - q // 2) % NZ)


def iota(shape, dim):
    return lax.broadcasted_iota(jnp.int32, shape, dim)


def slot_map():
    e, s = iota((128, 128), 0), iota((128, 128), 1)
    return ((s >= CAP * e) & (s < CAP * (e + 1)) & (e < NZ)).astype(f32).astype(bf16)


def weights_of(named, total):
    return jnp.where(named > 0.0, SCALE * named / total, 0.0).astype(bf16)


def router(logits_ref, ids_ref):
    rows = logits_ref.shape[0]
    ids = jnp.transpose(ids_ref[...].astype(f32))
    lanes = iota(logits_ref.shape, 1).astype(f32)
    hit = lanes == ids[:, 0:1]
    for k in range(1, ids.shape[1]):
        hit = hit | (lanes == ids[:, k : k + 1])
    named = jnp.where(hit, jax.nn.sigmoid(logits_ref[...]), 0.0)
    total = jnp.sum(named, axis=1, keepdims=True)
    held = named[:, :128]
    slots = slot_map()
    member = jnp.dot((held > 0.0).astype(f32).astype(bf16), slots, preferred_element_type=f32)
    spread = jnp.dot(weights_of(held, total), slots, preferred_element_type=f32)
    earlier = (iota((rows, rows), 0) > iota((rows, rows), 1)).astype(f32).astype(bf16)
    rank = jnp.dot(earlier, member.astype(bf16), preferred_element_type=f32)
    lane = iota((rows, 128), 1)
    first = jnp.zeros((rows, 128), jnp.int32)
    for j in range(1, NZ):
        first = first + CAP * (lane >= CAP * j).astype(jnp.int32)
    place = jnp.where(rank == (lane - first).astype(f32), member, 0.0)
    return named, total, place, place * spread


def kernel(
    logits_ref, ids_ref, tok_hbm, cot_hbm, gate_hbm, up_hbm, down_hbm,
    named_ref, total_ref, take_ref, fin, dg_hbm,
    tok, cot, sendb, rx, xr, cr, wg, wu, wd, relay_g, relay_u, relay_d,
    part, y1p, y1m, y2p, y2m, mid, bk, x1p, x1m, x2p, x2m,
    retb, dl, dt, dd, dsend, drecv, dout,
    lsem, wlsem, sem_a, sem_bp, sem_bm, sem_cp, sem_cm, wsem, rsem, psem,
    ysem, msem, xsem, fsem, ssem, dsem, osem, tsem,
):
    wide = xr.shape[1]
    half = wide // 2
    ffd = gate_hbm.shape[1]
    ff = wg.shape[1]
    rows = NS * CAP
    step = rows // NB
    batch = NX * step
    e = lax.axis_index("expert")
    c = lax.axis_index("dp")
    z, x, y = e // (NX * NY), (e // NY) % NX, e % NY
    other = 1 - c
    at = lambda zz, xx, yy: zz * (NX * NY) + xx * NY + yy
    yp, ym, y2 = (y + 1) % NY, (y + 3) % NY, (y + 2) % NY
    xp, xm, x2 = (x + 1) % NX, (x + 3) % NX, (x + 2) % NX
    dev_yp, dev_ym = at(z, x, yp), at(z, x, ym)
    dev_xp, dev_xm = at(z, xp, y), at(z, xm, y)
    dev_t = at(z, y, x)

    def remote(src, dst, recv, ex, dp=c):
        return pltpu.make_async_remote_copy(
            src_ref=src, dst_ref=dst, send_sem=ssem.at[0], recv_sem=recv,
            device_id=(ex, dp), device_id_type=MESH,
        )

    sent = []

    def send(src, dst, recv, ex, dp=c):
        cp = remote(src, dst, recv, ex, dp)
        cp.start()
        sent.append(cp)

    def arrived(dst, recv):
        remote(dst, dst, recv, dev_yp).wait_recv()

    ld_t = pltpu.make_async_copy(tok_hbm, tok, lsem.at[0])
    ld_c = pltpu.make_async_copy(cot_hbm, cot, lsem.at[1])
    ld_t.start()
    ld_c.start()

    barrier = pltpu.get_barrier_semaphore()

    def greet(ex, dp):
        pl.semaphore_signal(barrier, inc=1, device_id=(ex, dp), device_id_type=MESH)

    @pl.loop(1, NS)
    def _(d):
        greet(at((z + d // NY) % NZ, x, (y + d % NY) % NY), c)

    greet(dev_xp, c)
    greet(dev_xm, c)
    for d in range(NY):
        greet(at(z, x, (y + d) % NY), other)

    @pl.when(x != y)
    def _():
        greet(dev_t, c)

    r_own = pl.ds(pl.multiple_of(y * wide, wide), wide)
    l_own = pl.ds(pl.multiple_of(y * ffd, ffd), ffd)
    w_loads = [
        pltpu.make_async_copy(gate_hbm.at[r_own], wg.at[:, l_own], wlsem.at[0]),
        pltpu.make_async_copy(up_hbm.at[r_own], wu.at[:, l_own], wlsem.at[1]),
        pltpu.make_async_copy(down_hbm.at[:, r_own], wd.at[l_own], wlsem.at[2]),
    ]
    for cp in w_loads:
        cp.start()

    named, total, place, place_w = router(logits_ref, ids_ref)
    named_ref[...] = named
    total_ref[...] = jnp.broadcast_to(total, total_ref.shape)
    take_ref[...] = place.astype(bf16)
    put, put_w = place[:, :PAD].astype(bf16), place_w[:, :PAD].astype(bf16)
    pl.semaphore_wait(barrier, NS - 1 + 2 + NY + jnp.where(x == y, 0, 1))

    h = pl.ds(pl.multiple_of(c * half, half), half)

    def src_of(yy):
        r = pl.ds(pl.multiple_of(yy * wide + c * half, half), half)
        return (gate_hbm.at[r], up_hbm.at[r], down_hbm.at[:, r])

    def dst_of(yy, hh):
        l = pl.ds(pl.multiple_of(yy * ffd, ffd), ffd)
        return (wg.at[hh, l], wu.at[hh, l], wd.at[l, hh])

    relays = (relay_g, relay_u, relay_d)
    via = jnp.where(c == 0, dev_yp, dev_ym)
    came = jnp.where(c == 0, ym, yp)
    send(src_of(y2)[2], relays[2], rsem.at[2], via)
    ld_t.wait()
    ld_c.wait()
    for yy in range(NY):
        cols = slice(yy * wide, (yy + 1) * wide)
        v = lax.dot_general(put, tok[:, cols], TN, preferred_element_type=f32).astype(bf16)
        sendb[yy, 0] = v[:SLOTS].reshape(SLOTS, 2, half)
        v = lax.dot_general(put_w, cot[:, cols], TN, preferred_element_type=f32).astype(bf16)
        sendb[yy, 1] = v[:SLOTS].reshape(SLOTS, 2, half)

    def a_copy(d):
        q = d // NY
        zz, yy, s = (z + z_step(q)) % NZ, (y + d % NY) % NY, q * NY + y
        return remote(
            sendb.at[yy, :, pl.ds(zz * CAP, CAP)], rx.at[:, x, pl.ds(s * CAP, CAP)],
            sem_a.at[s], at(zz, x, yy),
        )

    own = pltpu.make_async_copy(
        sendb.at[y, :, pl.ds(z * CAP, CAP)], rx.at[:, x, pl.ds(y * CAP, CAP)], sem_a.at[y]
    )
    own.start()

    @pl.loop(1, NS)
    def _(d):
        a_copy(d).start()

    for i in (0, 1):
        send(src_of(y2)[i], relays[i], rsem.at[i], via)
    for i, s in enumerate(src_of(yp)):
        send(s, dst_of(y, h)[i], wsem.at[y, i], dev_yp)
    for i, s in enumerate(src_of(ym)):
        send(s, dst_of(y, h)[i], wsem.at[y, i], dev_ym)

    def src_at(d):
        s = (d // NY) * NY + (y + NY - d % NY) % NY
        return s, pl.ds(s * CAP, CAP)

    def b_copies(d):
        s, r = src_at(d)
        blk = rx.at[:, x, r]
        return remote(blk, blk, sem_bp.at[s], dev_xp), remote(blk, blk, sem_bm.at[s], dev_xm)

    def c_copies(d):
        s, r = src_at(d)
        pb, mb = rx.at[0, xm, r], rx.at[1, xp, r]
        return remote(pb, pb, sem_cp.at[s], dev_xp), remote(mb, mb, sem_cm.at[s], dev_xm)

    def start_b(d):
        for cp in b_copies(d):
            cp.start()

    def start_c(d):
        s, r = src_at(d)
        arrived(rx.at[:, xm, r], sem_bp.at[s])
        arrived(rx.at[:, xp, r], sem_bm.at[s])
        for cp in c_copies(d):
            cp.start()

    def wait_a(d):
        s, r = src_at(d)
        arrived(rx.at[:, x, r], sem_a.at[s])

    own.wait()
    start_b(0)

    @pl.loop(1, LAG)
    def _(d):
        wait_a(d)
        start_b(d)

    @pl.loop(LAG, 8)
    def _(d):
        wait_a(d)
        start_b(d)
        start_c(d - LAG)

    arrived(relays[2], rsem.at[2])
    send(relays[2], dst_of(came, h)[2], wsem.at[came, 2], via)

    @pl.loop(8, 14)
    def _(d):
        wait_a(d)
        start_b(d)
        start_c(d - LAG)

    arrived(relays[0], rsem.at[0])
    send(relays[0], dst_of(came, h)[0], wsem.at[came, 0], via)

    @pl.loop(14, 20)
    def _(d):
        wait_a(d)
        start_b(d)
        start_c(d - LAG)

    arrived(relays[1], rsem.at[1])
    send(relays[1], dst_of(came, h)[1], wsem.at[came, 1], via)

    @pl.loop(20, NS)
    def _(d):
        wait_a(d)
        start_b(d)
        start_c(d - LAG)


    def swap(yy):
        for i in range(3):
            blk = dst_of(yy, h)[i]
            arrived(blk, wsem.at[yy, i])
            send(blk, blk, psem.at[yy, i], e, other)

    @pl.loop(NS - LAG, NS)
    def _(d):
        start_c(d)

    swap(yp)
    swap(ym)


    def unpack(b):
        @pl.loop(0, step // 16)
        def _(i):
            o = pl.multiple_of(b * step + i * 16, 16)
            for k in range(NX):
                r = pl.ds(pl.multiple_of(b * batch + k * step + i * 16, 16), 16)
                xr[r] = rx[0, k, pl.ds(o, 16)].reshape(16, wide)
                cr[r] = rx[1, k, pl.ds(o, 16)].reshape(16, wide)

    def wait_c(b):
        @pl.loop(b * (NS // NB), (b + 1) * (NS // NB))
        def _(d):
            s, r = src_at(d)
            arrived(rx.at[0, x2, r], sem_cp.at[s])
            arrived(rx.at[1, x2, r], sem_cm.at[s])

    wait_c(0)
    unpack(0)

    swap(y2)
    ho = pl.ds(pl.multiple_of(other * half, half), half)
    for cp in w_loads:
        cp.wait()
    for yy in (yp, ym, y2):
        for i in range(3):
            arrived(dst_of(yy, ho)[i], psem.at[yy, i])

    def chunk(k, b):
        return pl.ds(pl.multiple_of(b * batch + k * step, 16), step)

    class Scatter:
        def __init__(self, part, pos, dev_p, dev_m, b1p, b1m, b2p, b2m, sems):
            self.part, self.pos = part, pos
            self.devs, self.bufs, self.sems = (dev_p, dev_m), (b1p, b1m, b2p, b2m), sems
            self.kp, self.km, self.kf = (pos + 1) % 4, (pos + 3) % 4, (pos + 2) % 4
            w = part.shape[1]
            self.lo, self.hi = slice(0, w // 2), slice(w // 2, w)

        def start(self, b):
            r = slice(b * step, (b + 1) * step)
            b1p, b1m, b2p, b2m = self.bufs
            (p, m), lo, hi, sem = self.devs, self.lo, self.hi, self.sems
            far, kp, km = chunk(self.kf, b), chunk(self.kp, b), chunk(self.km, b)
            send(self.part.at[far, lo], b1p.at[r], sem.at[b, 0], p)
            send(self.part.at[far, hi], b1m.at[r], sem.at[b, 1], m)
            send(self.part.at[kp, hi], b2p.at[r, hi], sem.at[b, 2], p)
            send(self.part.at[km, lo], b2m.at[r, lo], sem.at[b, 3], m)

        def onward(self, b):
            r = slice(b * step, (b + 1) * step)
            b1p, b1m, b2p, b2m = self.bufs
            (p, m), lo, hi, sem = self.devs, self.lo, self.hi, self.sems
            for buf, k, cols, i, to, dev in (
                (b1p, self.kp, lo, 0, b2p, p), (b1m, self.km, hi, 1, b2m, m),
            ):
                arrived(buf.at[r], sem.at[b, i])
                c = chunk(k, b)
                self.part[c, cols] = (self.part[c, cols].astype(f32) + buf[r].astype(f32)).astype(bf16)
                send(self.part.at[c, cols], to.at[r, cols], sem.at[b, 4 + i], dev)

        def finish(self, b):
            r = slice(b * step, (b + 1) * step)
            _, _, b2p, b2m = self.bufs
            arrived(b2p.at[r, self.hi], self.sems.at[b, 2])
            arrived(b2m.at[r, self.lo], self.sems.at[b, 3])
            arrived(b2p.at[r, self.lo], self.sems.at[b, 4])
            arrived(b2m.at[r, self.hi], self.sems.at[b, 5])

    def forward(b):
        r = slice(b * batch, (b + 1) * batch)
        part[r, 0:ff] = jnp.dot(xr[r], wg[...], preferred_element_type=f32).astype(bf16)
        part[r, ff : 2 * ff] = jnp.dot(xr[r], wu[...], preferred_element_type=f32).astype(bf16)
        part[r, 2 * ff : 3 * ff] = lax.dot_general(
            cr[r], wd[...], NT, preferred_element_type=f32
        ).astype(bf16)

    def activate(b):
        @pl.loop(0, step // 16)
        def _(i):
            r = pl.ds(pl.multiple_of(b * step + i * 16, 16), 16)
            mr = pl.ds(pl.multiple_of(b * batch + y * step + i * 16, 16), 16)
            full = part[mr].astype(f32) + y2p[r].astype(f32) + y2m[r].astype(f32)
            g, u, pw = full[:, :ff], full[:, ff : 2 * ff], full[:, 2 * ff :]
            sig = jax.nn.sigmoid(g)
            act = g * sig
            hid = (act * u).astype(bf16)
            prod = hid.astype(f32) * pw
            lanes = prod[:, :128]
            for k in range(1, ff // 128):
                lanes = lanes + prod[:, k * 128 : (k + 1) * 128]
            mid[mr, 2 * ff : 3 * ff] = hid
            mid[mr, 0:ff] = (pw * u * sig * (1.0 + g * (1.0 - sig))).astype(bf16)
            mid[mr, ff : 2 * ff] = (pw * act).astype(bf16)
            top = lanes.astype(bf16)
            low = lanes - top.astype(f32)
            both = jnp.concatenate([top.astype(f32), low], axis=1).astype(bf16)
            dl[pl.ds(b * step + i * 16, 16)] = both.reshape(16, 2, 128)

    gather_cols = (
        (slice(0, ff), slice(ff, 2 * ff)),
        (slice(2 * ff, 5 * ff // 2), slice(5 * ff // 2, 3 * ff)),
    )

    def block(k, b, cols):
        return mid.at[chunk(k, b), cols]

    def gather_start(b, g):
        lo, hi = gather_cols[g]
        for i, (cols, dev) in enumerate(((lo, dev_yp), (hi, dev_ym), (hi, dev_yp), (lo, dev_ym))):
            send(block(y, b, cols), block(y, b, cols), msem.at[b, 6 * g + i], dev)

    def gather_onward(b, g):
        lo, hi = gather_cols[g]
        arrived(block(ym, b, lo), msem.at[b, 6 * g])
        send(block(ym, b, lo), block(ym, b, lo), msem.at[b, 6 * g + 4], dev_yp)
        arrived(block(yp, b, hi), msem.at[b, 6 * g + 1])
        send(block(yp, b, hi), block(yp, b, hi), msem.at[b, 6 * g + 5], dev_ym)

    def gather_finish(b, g):
        lo, hi = gather_cols[g]
        arrived(block(ym, b, hi), msem.at[b, 6 * g + 2])
        arrived(block(yp, b, lo), msem.at[b, 6 * g + 3])
        arrived(block(y2, b, lo), msem.at[b, 6 * g + 4])
        arrived(block(y2, b, hi), msem.at[b, 6 * g + 5])

    def backward(b):
        r = slice(b * batch, (b + 1) * batch)
        v = lax.dot_general(mid[r, 0:ff], wg[...], NT, preferred_element_type=f32)
        v = v + lax.dot_general(mid[r, ff : 2 * ff], wu[...], NT, preferred_element_type=f32)
        bk[r] = v.astype(bf16)

    def home(b):
        @pl.loop(0, step // 16)
        def _(i):
            o = pl.multiple_of(b * step + i * 16, 16)
            r = pl.ds(o, 16)
            mr = pl.ds(pl.multiple_of(b * batch + x * step + i * 16, 16), 16)
            full = bk[mr].astype(f32) + x2p[r].astype(f32) + x2m[r].astype(f32)
            retb[r, :, 0:half] = full.astype(bf16).reshape(16, 2, half)
            retb[r, :, half : half + 128] = dt[r]

        lo, hi = b * (NS // NB), (b + 1) * (NS // NB)

        @pl.loop(max(lo, 1), hi)
        def _(d):
            f_copy(d).start()

    def f_copy(d):
        s, r = src_at(d)
        return remote(
            retb.at[r], fin.at[y, pl.ds(z * CAP, CAP)], fsem.at[z * NY + y],
            at((z + NZ - z_step(d // NY)) % NZ, x, (y + NY - d % NY) % NY),
        )

    mine = pl.ds(pl.multiple_of(c * (ff // 2), ff // 2), ff // 2)
    theirs = pl.ds(pl.multiple_of(other * (ff // 2), ff // 2), ff // 2)
    to_core = y // 2
    o_cols = pl.ds(pl.multiple_of((y % 2) * wide, wide), wide)

    def out_copy(i):
        return remote(
            dout.at[pl.ds(i * ffd, ffd)], dg_hbm.at[0, :, o_cols], osem.at[y % 2],
            at(z, x, 2 * c + i), to_core,
        )

    def down_half(b):
        r = slice(b * batch, (b + 1) * batch)
        v = lax.dot_general(mid[r, 2 * ff : 3 * ff], cr[r], TN, preferred_element_type=f32)
        dd[...] = v if b == batches[0] else dd[...] + v

    fwd = Scatter(part, y, dev_yp, dev_ym, y1p, y1m, y2p, y2m, ysem)
    bwd = Scatter(bk, x, dev_xp, dev_xm, x1p, x1m, x2p, x2m, xsem)
    batches = tuple(range(NB))

    forward(0)
    fwd.start(0)
    wait_c(1)
    unpack(1)
    forward(1)
    fwd.onward(0)
    fwd.start(1)
    fwd.onward(1)
    for b in batches:
        fwd.finish(b)
        activate(b)
        gather_start(b, 0)

    dots_here = pltpu.make_async_copy(dl, dt, tsem.at[0])
    dots_there = remote(dl, dt, tsem.at[0], dev_t)

    @pl.when(x == y)
    def _():
        dots_here.start()

    @pl.when(x != y)
    def _():
        dots_there.start()

    gather_onward(0, 0)
    gather_start(0, 1)
    gather_onward(1, 0)
    gather_start(1, 1)
    gather_finish(0, 0)
    backward(0)
    bwd.start(0)
    gather_onward(0, 1)
    gather_finish(1, 0)
    backward(1)
    bwd.onward(0)
    bwd.start(1)
    gather_onward(1, 1)
    gather_finish(0, 1)
    down_half(0)
    gather_finish(1, 1)
    down_half(1)
    dsend[...] = dd[theirs].astype(bf16)
    send(dsend, drecv, dsem.at[0], e, other)
    arrived(dt, tsem.at[0])
    bwd.onward(1)
    bwd.finish(0)
    home(0)
    arrived(drecv, dsem.at[0])
    dout[...] = (dd[mine] + drecv[...].astype(f32)).astype(bf16)
    for i in range(2):
        here = (2 * c + i == y) & (to_core == c)

        @pl.when(here)
        def _():
            pltpu.make_async_copy(
                dout.at[pl.ds(i * ffd, ffd)], dg_hbm.at[0, :, o_cols], osem.at[y % 2]
            ).start()

        @pl.when(jnp.logical_not(here))
        def _():
            out_copy(i).start()

    bwd.finish(1)
    home(1)

    back_own = pltpu.make_async_copy(
        retb.at[pl.ds(y * CAP, CAP)], fin.at[y, pl.ds(z * CAP, CAP)], fsem.at[z * NY + y]
    )
    back_own.start()
    back_own.wait()

    @pl.loop(1, NS)
    def _(d):
        zz, yy = (z + d // NY) % NZ, (y + d % NY) % NY
        arrived(fin.at[yy, pl.ds(zz * CAP, CAP)], fsem.at[zz * NY + yy])

    @pl.loop(1, NS)
    def _(d):
        f_copy(d).wait_send()

    for cp in sent:
        cp.wait_send()

    @pl.loop(1, NS)
    def _(d):
        a_copy(d).wait_send()

    @pl.loop(0, NS)
    def _(d):
        for cp in (*b_copies(d), *c_copies(d)):
            cp.wait_send()

    @pl.when(x != y)
    def _():
        dots_there.wait_send()

    for i in range(2):
        arrived(dg_hbm.at[0, :, i * wide : (i + 1) * wide], osem.at[i])

        @pl.when(jnp.logical_not((2 * c + i == y) & (to_core == c)))
        def _():
            out_copy(i).wait_send()


def exchange(logits, ids, tokens, cotangent, gate, up, down):
    tok_count, width = tokens.shape
    ffd = gate.shape[1]
    wide, ff, rows = width // NY, NY * ffd, NS * CAP
    half = wide // 2
    n = NX * rows
    vm = pltpu.VMEM
    dma = pltpu.SemaphoreType.DMA
    scratch = [
        vm((tok_count, width), bf16), vm((tok_count, width), bf16),
        vm((NY, 2, SLOTS, 2, half), bf16), vm((2, NX, rows, 2, half), bf16),
        vm((n, wide), bf16), vm((n, wide), bf16),
        vm((wide, ff), bf16), vm((wide, ff), bf16), vm((ff, wide), bf16),
        vm((half, ffd), bf16), vm((half, ffd), bf16), vm((ffd, half), bf16),
        vm((n, 3 * ff), bf16),
        vm((rows, 3 * ff // 2), bf16), vm((rows, 3 * ff // 2), bf16),
        vm((rows, 3 * ff), bf16), vm((rows, 3 * ff), bf16),
        vm((n, 3 * ff), bf16),
        vm((n, wide), bf16),
        vm((rows, half), bf16), vm((rows, half), bf16),
        vm((rows, wide), bf16), vm((rows, wide), bf16),
        vm((rows, 2, half + 128), bf16), vm((rows, 2, 128), bf16), vm((rows, 2, 128), bf16),
        vm((ff, wide), f32), vm((ff // 2, wide), bf16), vm((ff // 2, wide), bf16), vm((ff // 2, wide), bf16),
        dma((2,)), dma((3,)), dma((NS,)), dma((NS,)), dma((NS,)), dma((NS,)), dma((NS,)),
        dma((NY, 3)), dma((3,)), dma((NY, 3)),
        dma((NB, 6)), dma((NB, 12)), dma((NB, 6)), dma((NS,)), dma((1,)), dma((1,)), dma((2,)), dma((1,)),
    ]
    v, a = pl.BlockSpec(memory_space=pltpu.VMEM), pl.BlockSpec(memory_space=pl.ANY)
    return pl.pallas_call(
        kernel,
        out_shape=(
            jax.ShapeDtypeStruct(logits.shape, f32),
            jax.ShapeDtypeStruct((tok_count, 128), f32),
            jax.ShapeDtypeStruct((tok_count, 128), bf16),
            jax.ShapeDtypeStruct((NY, SLOTS, 2, half + 128), bf16),
            jax.ShapeDtypeStruct((1, ffd, width // 2), bf16),
        ),
        in_specs=[v, v, a, a, a, a, a],
        out_specs=(v, v, v, a, a),
        scratch_shapes=scratch,
        compiler_params=pltpu.CompilerParams(
            collective_id=0, has_side_effects=True, vmem_limit_bytes=62 * 1024 * 1024
        ),
        name="exchange",
    )(logits, ids, tokens, cotangent, gate, up, down)


def closing(named_ref, total_ref, take_ref, fin_ref, dg_in, tg_ref, lg_ref, dg_ref, acc):
    b = pl.program_id(0)
    half = fin_ref.shape[3] - 128
    dg_ref[...] = dg_in[...]
    v = fin_ref[0, :, :, 0:half].reshape(SLOTS, 2 * half)
    tg_ref[...] = jnp.dot(take_ref[:, :SLOTS], v, preferred_element_type=f32).astype(bf16)
    d = fin_ref[0, :, :, half : half + 128].reshape(SLOTS, 256).astype(f32)
    d = d[:, :128] + d[:, 128:]

    @pl.when(b == 0)
    def _():
        acc[...] = d

    @pl.when(b > 0)
    def _():
        acc[...] += d

    @pl.when(b == NY - 1)
    def _():
        dots = jnp.broadcast_to(jnp.sum(acc[...], axis=1, keepdims=True), (SLOTS, 128))
        top = dots.astype(bf16)
        low = (dots - top.astype(f32)).astype(bf16)
        slots = jnp.transpose(slot_map().astype(f32))[:SLOTS].astype(bf16)
        take = take_ref[:, :SLOTS]
        got = jnp.dot(take, slots * top, preferred_element_type=f32)
        got = got + jnp.dot(take, slots * low, preferred_element_type=f32)
        named, total = named_ref[...], total_ref[:, 0:1]
        held = named[:, :128]
        weight = weights_of(held, total).astype(f32)
        dweight = jnp.where(weight > 0.0, got / jnp.where(weight > 0.0, weight, 1.0), 0.0)
        inner = jnp.sum(dweight * held, axis=1, keepdims=True) / total
        rest = named[:, 128:]
        scale = SCALE / total
        lg_ref[:, :128] = scale * (dweight - inner) * held * (1.0 - held)
        lg_ref[:, 128:] = scale * (0.0 - inner) * rest * (1.0 - rest)


def per_device(tokens, cotangent, logits, expert_ids, gate_proj, up_proj, down_proj):
    tok_count, width = tokens.shape
    wide = width // NY
    ids = expert_ids.T
    ffd = gate_proj.shape[2]
    named, total, take, fin, dg = exchange(
        logits, ids, tokens, cotangent, gate_proj[0], up_proj[0], down_proj[0]
    )
    whole = lambda s: pl.BlockSpec(s, lambda b: (0,) * len(s))
    return pl.pallas_call(
        closing,
        grid=(NY,),
        out_shape=(
            jax.ShapeDtypeStruct(tokens.shape, bf16),
            jax.ShapeDtypeStruct(logits.shape, f32),
            jax.ShapeDtypeStruct(dg.shape, bf16),
        ),
        in_specs=[
            whole(named.shape), whole(total.shape), whole(take.shape),
            pl.BlockSpec((1,) + fin.shape[1:], lambda b: (b, 0, 0, 0)),
            pl.BlockSpec((1, ffd, wide // 2), lambda b: (0, 0, b)),
        ],
        out_specs=(
            pl.BlockSpec((tok_count, wide), lambda b: (0, b)),
            whole(logits.shape),
            pl.BlockSpec((1, ffd, wide // 2), lambda b: (0, 0, b)),
        ),
        scratch_shapes=[pltpu.VMEM((SLOTS, 128), f32)],
        name="closing",
    )(named, total, take, fin, dg)


def solution(mesh):
    rows = P(("expert", "dp"), None)
    mats = P("expert", None, None)
    return jax.shard_map(
        per_device,
        mesh=mesh,
        in_specs=(rows, rows, rows, rows, mats, mats, mats),
        out_specs=(rows, rows, P("expert", None, "dp")),
        check_vma=False,
    )
```
